32 devices in a mesh: inst: 4 (over y, x), row: 2 (over core), pitch: 4 (over z).
Axes of the slice: x: 2, y: 2, z: 4, core: 2. Of those that a mesh axis runs over, the one named last changes fastest.
Arguments:
- direction: float32 [4, 5, 12288], P('inst', None, ('row', 'pitch')), may hold values from -6 to 6
- time_matrix: float32 [4, 4], replicated, may hold values from -3 to 3
- volume: float32 [12288], P(('row', 'pitch')), may hold values from 0.5 to 2
- diag_jac: float32 [4, 25, 12288], P('inst', None, ('row', 'pitch')), may hold values from -2.5 to 2.5
- face_jac: float32 [4, 50, 24576], P('inst', None, ('row', 'pitch')), may hold values from -1 to 1
- face_left: int32 [24576], P(('row', 'pitch')), may hold values from 0 to 1535
- face_right: int32 [24576], P(('row', 'pitch')), may hold values from 0 to 1535
- bound_jac: float32 [4, 4, 50, 3072], P('inst', None, None, ('row', 'pitch')), may hold values from -1 to 1
- bound_cell: int32 [4, 3072], P(None, ('row', 'pitch')), may hold values from 0 to 1535
- send_cell: int32 [4, 3072], P(None, ('row', 'pitch')), may hold values from 0 to 1535
Outputs:
- product: float32 [4, 5, 12288], P('inst', None, ('row', 'pitch'))
The draws below stay inside these ranges and needn't reach their ends.
Inputs may be any that keep to these rules, and one draw needn't show every extreme that they name: `face_left`: a cell index local to the face's block of 1536 cells. `face_right`: a cell index local to the face's block of 1536 cells. `bound_cell`: a cell index local to the face's block of 1536 cells. `send_cell`: a cell index local to the supplying block of 1536 cells.
All inputs are finite; a program needn't handle non-finite values.
Results may differ from the reference program's by a relative error of at most 0.000052.
Values sent between devices are 32-bit elements; how exact they have to be, the bound alone decides.
A program may use at most 128 MiB of HBM per device.

```python
import math
import jax
import jax.numpy as jnp
from jax import lax

CELL_DEV = 1536
NT = 4
COMP = 5
FACE_DEV = 3072
BND_DEV = 384
CELLS = 12288
FACES = 24576
BOUNDS = 3072
N_ROW = 2
N_PITCH = 4


def plant(values, stream_key, smallest, largest):
    shape = values.shape
    place = [jax.random.randint(jax.random.fold_in(stream_key, axis), (), 0, shape[axis]) for axis in range(len(shape))]
    values = values.at[tuple(place)].set(smallest)
    longest = shape.index(max(shape))
    place[longest] = (place[longest] + 1) % shape[longest]
    return values.at[tuple(place)].set(largest)


def block_levels(own_key, shape, cuts, least, top_value):
    level = 1.0
    for axis_at, parts in cuts:
        draws = jax.random.uniform(jax.random.fold_in(jax.random.fold_in(own_key, 6), axis_at), (parts,), jnp.float32, least / len(cuts), top_value / len(cuts))
        level = level * jnp.repeat(jnp.exp(draws), shape[axis_at] // parts).reshape((-1,) + (1,) * (len(shape) - 1 - axis_at))
    return level


def bell_draw(own_key, shape, width, limit, pieces=(), kind=jnp.bfloat16):
    values = width * jax.random.normal(own_key, shape, jnp.float32)
    if pieces:
        values = values * block_levels(own_key, shape, pieces, -0.22, 0.18)
    return jnp.clip(values, -limit, limit).astype(kind)


def setup_inputs(seed: int = 0) -> dict:
    streams_of = jax.random.split(jax.random.key(seed), 11)
    return {
        "direction": bell_draw(streams_of[0], (NT, COMP, CELLS), 1.0, 6.0, ((0, 4), (2, 8)), jnp.float32),
        "time_matrix": bell_draw(streams_of[1], (NT, NT), NT ** -0.5, 3.0, (), jnp.float32),
        "volume": jnp.clip(jnp.exp(math.log(2.0) - 1.3862944 * jax.random.uniform(streams_of[2], (CELLS,), jnp.float32) ** block_levels(streams_of[2], (CELLS,), ((0, 8),), -0.2, 0.2)), 0.5, 2.0),
        "diag_jac": bell_draw(streams_of[3], (NT, COMP * COMP, CELLS), 5 ** -0.5, 2.5, ((0, 4), (2, 8)), jnp.float32),
        "face_jac": bell_draw(streams_of[4], (NT, 2 * COMP * COMP, FACES), 30 ** -0.5, 1.0, ((0, 4), (2, 8)), jnp.float32),
        "face_left": plant(jax.random.randint(streams_of[5], (FACES,), 0, CELL_DEV), jax.random.fold_in(streams_of[5], 1), 0, CELL_DEV - 1).astype(jnp.int32),
        "face_right": plant(jax.random.randint(streams_of[6], (FACES,), 0, CELL_DEV), jax.random.fold_in(streams_of[6], 1), 0, CELL_DEV - 1).astype(jnp.int32),
        "bound_jac": bell_draw(streams_of[7], (NT, 4, 2 * COMP * COMP, BOUNDS), 30 ** -0.5, 1.0, ((0, 4), (3, 8)), jnp.float32),
        "bound_cell": plant(jax.random.randint(streams_of[8], (4, BOUNDS), 0, CELL_DEV), jax.random.fold_in(streams_of[8], 1), 0, CELL_DEV - 1).astype(jnp.int32),
        "send_cell": plant(jax.random.randint(streams_of[9], (4, BOUNDS), 0, CELL_DEV), jax.random.fold_in(streams_of[9], 1), 0, CELL_DEV - 1).astype(jnp.int32),
    }


def reference(direction, time_matrix, volume, diag_jac, face_jac, face_left, face_right, bound_jac, bound_cell, send_cell):
    high = lax.Precision.HIGHEST
    spectral = jnp.einsum('ij,jcx->icx', time_matrix, direction, precision=high) * volume[None, None, :]
    blocks = diag_jac.reshape(NT, 5, 5, CELLS)
    result = spectral + jnp.einsum('tabx,tbx->tax', blocks, direction, precision=high)
    offset = (jnp.arange(FACES, dtype=jnp.int32) // FACE_DEV) * CELL_DEV
    left_cell = (face_left + offset).astype(jnp.int32)
    right_cell = (face_right + offset).astype(jnp.int32)
    pair = face_jac.reshape(NT, 2, 5, 5, FACES)
    flux = jnp.einsum('tabf,tbf->taf', pair[:, 0], direction[:, :, left_cell], precision=high)
    flux = flux + jnp.einsum('tabf,tbf->taf', pair[:, 1], direction[:, :, right_cell], precision=high)
    result = result.at[:, :, left_cell].add(flux).at[:, :, right_cell].add(-flux)
    bound_offset = (jnp.arange(BOUNDS, dtype=jnp.int32) // BND_DEV) * CELL_DEV
    own_cell = (bound_cell + bound_offset[None, :]).astype(jnp.int32)
    sent_cell = (send_cell + bound_offset[None, :]).astype(jnp.int32)
    sent = direction[:, :, sent_cell].reshape(NT, 5, 4, N_ROW, N_PITCH, BND_DEV)
    ghost_low = jnp.roll(sent[:, :, 1], 1, axis=3)
    ghost_high = jnp.roll(sent[:, :, 0], -1, axis=3)
    zero_rim = jnp.zeros((NT, 5, 1, N_PITCH, BND_DEV), jnp.float32)
    ghost_below = jnp.concatenate([zero_rim, sent[:, :, 3][:, :, :-1]], axis=2)
    ghost_above = jnp.concatenate([sent[:, :, 2][:, :, 1:], zero_rim], axis=2)
    ghosts = jnp.stack([ghost_low, ghost_high, ghost_below, ghost_above], axis=2).reshape(NT, 5, 4, BOUNDS)
    inner = direction[:, :, own_cell]
    bound_pair = bound_jac.reshape(NT, 4, 2, 5, 5, BOUNDS)
    bound_flux = jnp.einsum('tkabx,tbkx->takx', bound_pair[:, :, 0], inner, precision=high)
    bound_flux = bound_flux + jnp.einsum('tkabx,tbkx->takx', bound_pair[:, :, 1], ghosts, precision=high)
    result = result.at[:, :, own_cell.reshape(-1)].add(bound_flux.reshape(NT, 5, 4 * BOUNDS))
    return result
```

```python
import functools
import jax
import jax.numpy as jnp
from jax import lax
from jax.experimental import pallas as pl
from jax.experimental.pallas import tpu as pltpu
from jax.sharding import PartitionSpec as P

LANE = 128
COMP = 5
TERMS = 2 * COMP
PACK = 16
GROUP = 4
MESH = pl.DeviceIdType.MESH


def gathered(own, cell):
    low = cell & (LANE - 1)
    high = cell >> 7
    chunks = own.shape[1] * GROUP
    masks = [high == h for h in range(chunks)]
    values = []
    for b in range(COMP):
        found = None
        for h in range(chunks):
            row = own[b, h // GROUP, pl.ds(h % GROUP, 1), :]
            part = jnp.take_along_axis(
                jnp.broadcast_to(row, cell.shape), low, axis=1, mode="promise_in_bounds"
            )
            found = part if h == 0 else jnp.where(masks[h], part, found)
        values.append(found)
    return values


def applied(block, base, values):
    result = []
    for a in range(COMP):
        total = None
        for b in range(COMP):
            term = block(base + COMP * a + b) * values[b]
            total = term if total is None else total + term
        result.append(total)
    return result


def two_terms(value):
    first = value.astype(jnp.bfloat16).astype(jnp.float32)
    return first, value - first


def packed_row(row):
    return jnp.broadcast_to(row, (PACK, LANE)).astype(jnp.bfloat16)


def hot_tile(hot, place, cell_row, value):
    low = packed_row((cell_row & (LANE - 1)).astype(jnp.float32))
    for s in range(0, LANE, PACK):
        index = lax.broadcasted_iota(jnp.int32, (PACK, LANE), 0) + s
        index = index.astype(jnp.float32).astype(jnp.bfloat16)
        hot[s : s + PACK, place : place + LANE] = jnp.where(
            index == low, jnp.bfloat16(value), jnp.bfloat16(0)
        )


def chunk_mask(cell_row):
    index = lax.broadcasted_iota(jnp.int32, (PACK, LANE), 0)
    index = index.astype(jnp.float32).astype(jnp.bfloat16)
    return index == packed_row((cell_row >> 7).astype(jnp.float32))


NEAR, LATE, BELOW, ABOVE = 0, 1, 2, 3


def kernel(n_inst, n_row, n_pitch, *refs):
    pl.run_scoped(
        functools.partial(body, n_inst, n_row, n_pitch, *refs),
        pltpu.SemaphoreType.DMA((10,)),
        pltpu.SemaphoreType.DMA((n_inst + 8,)),
    )


def body(
    n_inst,
    n_row,
    n_pitch,
    tm_hbm,
    dir_hbm,
    vol_hbm,
    diag_hbm,
    face_hbm,
    left_hbm,
    right_hbm,
    bound_hbm,
    bcell_hbm,
    scell_hbm,
    out_ref,
    tm_ref,
    own,
    vol_line,
    vol,
    diag,
    face,
    left,
    right,
    bound,
    bcell,
    dirs,
    ghost,
    ghost_cell,
    late_jac,
    inner_flux,
    place_cell,
    flux_terms,
    bound_terms,
    rows,
    hot,
    acc,
    inst_recv,
    ghost_recv,
    ready,
    local_sem,
    send_sem,
):
    t = lax.axis_index("inst")
    r = lax.axis_index("row")
    p = lax.axis_index("pitch")
    blocks = own.shape[1]
    chunks = blocks * GROUP
    f_tiles = left.shape[0]
    faces = f_tiles * LANE
    b_tiles = bcell.shape[0]
    bounds = b_tiles * LANE
    last = n_inst - 1

    barrier = pltpu.get_barrier_semaphore()

    def signal(sem, **place):
        pl.semaphore_signal(sem, inc=1, device_id=place, device_id_type=MESH)

    up = lax.rem(p + 1, n_pitch)
    down = lax.rem(p + n_pitch - 1, n_pitch)

    down_first = jnp.logical_and(p >= 1, p <= n_pitch - 2)
    up_first = p >= n_pitch - 2

    @pl.when(jnp.logical_not(down_first))
    def _():
        signal(barrier, pitch=down)

    @pl.when(jnp.logical_not(up_first))
    def _():
        signal(barrier, pitch=up)

    @pl.when(r < n_row - 1)
    def _():
        signal(barrier, row=r + 1)

    @pl.when(t == 0)
    def _():
        for u in range(1, n_inst):
            signal(barrier, inst=u)

    @pl.when(jnp.logical_and(t > 0, t < last))
    def _():
        signal(barrier, inst=last)

    pairs = [
        (dir_hbm, own),
        (bcell_hbm, bcell),
        (left_hbm, left),
        (right_hbm, right),
        (face_hbm, face),
        (bound_hbm, bound),
        (diag_hbm, diag),
        (vol_hbm, vol_line),
        (tm_hbm, tm_ref),
    ]
    copies = [
        pltpu.make_async_copy(a, b, local_sem.at[i]) for i, (a, b) in enumerate(pairs)
    ]

    def ghost_copies(slot, at, **place):
        return [
            pltpu.make_async_remote_copy(
                src_ref=a,
                dst_ref=b,
                send_sem=send_sem.at[at + i],
                recv_sem=ghost_recv.at[slot],
                device_id=place,
                device_id_type=MESH,
            )
            for i, (a, b) in enumerate(
                [(dir_hbm, ghost.at[slot, 0:COMP]), (scell_hbm, ghost_cell.at[slot])]
            )
        ]

    def to_up():
        return ghost_copies(jnp.where(p == n_pitch - 1, LATE, NEAR), n_inst, pitch=up)

    def to_down():
        return ghost_copies(jnp.where(p == 1, NEAR, LATE), n_inst + 2, pitch=down)

    def to_below():
        return ghost_copies(ABOVE, n_inst + 4, row=r - 1)

    def to_above():
        return ghost_copies(BELOW, n_inst + 6, row=r + 1)

    def start(group):
        for c in group:
            c.start()

    def inst_copy(o):
        return pltpu.make_async_remote_copy(
            src_ref=dir_hbm,
            dst_ref=dirs.at[o],
            send_sem=send_sem.at[o],
            recv_sem=inst_recv.at[0],
            device_id={"inst": lax.rem(t + o, n_inst)},
            device_id_type=MESH,
        )

    def inst_first(o):
        return jnp.logical_or(lax.rem(t + o, n_inst) == 0, t == last)

    greeted = jnp.where(t == last, last, jnp.where(t > 0, 1, 0))
    greeted = greeted + jnp.where(r > 0, 1, 0)
    greeted = greeted + jnp.where(down_first, 1, 0) + jnp.where(up_first, 1, 0)

    @pl.when(greeted > 0)
    def _():
        pl.semaphore_wait(barrier, greeted)

    @pl.when(up_first)
    def _():
        start(to_up())
        signal(ready.at[2], pitch=up)

    for o in range(1, n_inst):

        @pl.when(inst_first(o))
        def _(o=o):
            inst_copy(o).start()
            signal(ready.at[0], inst=lax.rem(t + o, n_inst))

    @pl.when(down_first)
    def _():
        start(to_down())
        signal(ready.at[1], pitch=down)

    @pl.when(r > 0)
    def _():
        start(to_below())
        signal(ready.at[0], row=r - 1)

    start(copies)

    @pl.when(r == 0)
    def _():
        ghost[BELOW] = jnp.zeros(ghost.shape[1:], jnp.float32)
        ghost_cell[BELOW] = jnp.zeros(ghost_cell.shape[1:], jnp.int32)

    @pl.when(r == n_row - 1)
    def _():
        ghost[ABOVE] = jnp.zeros(ghost.shape[1:], jnp.float32)
        ghost_cell[ABOVE] = jnp.zeros(ghost_cell.shape[1:], jnp.int32)

    for c in copies:
        c.wait()

    def product(start, size):
        return lax.dot_general(
            rows[:, start : start + size],
            hot[:, start : start + size],
            (((1,), (1,)), ((), ())),
            preferred_element_type=jnp.float32,
        )

    total = None
    for g in range(0, f_tiles, 8):
        block = lambda i, g=g: face[i, g : g + 8, :]
        cell_l = left[g : g + 8, :]
        cell_r = right[g : g + 8, :]
        one = applied(block, 0, gathered(own, cell_l))
        two = applied(block, COMP * COMP, gathered(own, cell_r))
        for a in range(COMP):
            first, rest = two_terms(one[a] + two[a])
            flux_terms[a, g : g + 8, :] = first
            flux_terms[COMP + a, g : g + 8, :] = rest
        for s in range(g, g + 8):
            place = 2 * s * LANE
            row_l = left[s : s + 1, :]
            row_r = right[s : s + 1, :]
            hot_tile(hot, place, row_l, 1.0)
            hot_tile(hot, place + LANE, row_r, -1.0)
            mask_l = chunk_mask(row_l)
            mask_r = chunk_mask(row_r)
            for a in range(TERMS):
                value = packed_row(flux_terms[a, s : s + 1, :])
                at = slice(a * PACK, (a + 1) * PACK)
                zero = jnp.bfloat16(0)
                rows[at, place : place + LANE] = jnp.where(mask_l, value, zero)
                rows[at, place + LANE : place + 2 * LANE] = jnp.where(mask_r, value, zero)
        part = product(2 * g * LANE, 16 * LANE)
        total = part if total is None else total + part
    acc[...] = total

    edge = p == 0

    def side(slot, pick):
        if slot >= BELOW:
            return pick(slot)
        if slot == NEAR:
            return jnp.where(edge, pick(1), pick(0))
        return jnp.where(edge, pick(0), pick(1))

    def boundary_place(slot, j):
        return 2 * faces + ((3 - slot) * b_tiles + j) * LANE

    for j in range(b_tiles):
        block = lambda i, j=j: bound[i, j]
        flux = applied(block, 0, gathered(own, bcell[j]))
        for a in range(COMP):
            inner_flux[a, j] = flux[a]
    for slot in range(4):
        place_cell[slot] = side(slot, lambda k: bcell[:, k, :])
        for j in range(b_tiles):
            hot_tile(hot, boundary_place(slot, j), place_cell[slot, j : j + 1, :], 1.0)
    for i in range(COMP * COMP):
        late_jac[i] = side(LATE, lambda k, i=i: bound[COMP * COMP + i, :, k, :])

    for h in range(chunks):
        vol[h // GROUP, pl.ds(h % GROUP, 1), :] = vol_line[
            h * LANE : (h + 1) * LANE
        ].reshape(1, LANE)

    for q in range(blocks):
        local = applied(lambda i, q=q: diag[i, q], 0, [own[b, q] for b in range(COMP)])
        for a in range(COMP):
            out_ref[a, q] = local[a] + (tm_ref[t, t] * own[a, q]) * vol[q]

    answered = jnp.where(t == 0, last, jnp.where(t < last, 1, 0))
    answered = answered + jnp.where(r < n_row - 1, 1, 0)

    @pl.when(answered > 0)
    def _():
        pl.semaphore_wait(ready.at[0], answered)

    for o in range(1, n_inst):

        @pl.when(jnp.logical_not(inst_first(o)))
        def _(o=o):
            inst_copy(o).start()

    @pl.when(r < n_row - 1)
    def _():
        start(to_above())

    @pl.when(jnp.logical_not(up_first))
    def _():
        pl.semaphore_wait(ready.at[1], 1)
        start(to_up())

    @pl.when(jnp.logical_not(down_first))
    def _():
        pl.semaphore_wait(ready.at[2], 1)
        start(to_down())

    def arrived(slot):
        pltpu.make_async_copy(ghost.at[slot], ghost.at[slot], ghost_recv.at[slot]).wait()

    def boundary(slot):
        cell = side(slot, lambda k: ghost_cell[slot, :, k ^ 1, :])
        values = gathered(ghost.at[slot], cell)
        if slot == LATE:
            block = lambda i: late_jac[i - COMP * COMP]
        else:
            block = lambda i: side(slot, lambda k: bound[i, :, k, :])
        flux = applied(block, COMP * COMP, values)
        for a in range(COMP):
            inner = side(slot, lambda k, a=a: inner_flux[a, :, k, :])
            first, rest = two_terms(inner + flux[a])
            bound_terms[slot, a] = first
            bound_terms[slot, COMP + a] = rest
        for j in range(b_tiles):
            place = boundary_place(slot, j)
            mask = chunk_mask(place_cell[slot, j : j + 1, :])
            for a in range(TERMS):
                value = packed_row(bound_terms[slot, a, j : j + 1, :])
                rows[a * PACK : (a + 1) * PACK, place : place + LANE] = jnp.where(
                    mask, value, jnp.bfloat16(0)
                )

    @pl.when(r > 0)
    def _():
        arrived(BELOW)

    @pl.when(r < n_row - 1)
    def _():
        arrived(ABOVE)

    boundary(ABOVE)
    boundary(BELOW)
    acc[...] = acc[...] + product(2 * faces, 2 * bounds)

    arrived(NEAR)
    boundary(NEAR)
    acc[...] = acc[...] + product(boundary_place(NEAR, 0), bounds)

    if n_inst > 1:
        others = dirs.at[1:n_inst]
        pltpu.make_async_copy(others, others, inst_recv.at[0]).wait()
    weights = [tm_ref[t, lax.rem(t + n_inst - o, n_inst)] for o in range(1, n_inst)]
    for q in range(blocks):
        for a in range(COMP):
            at = a * PACK + q * GROUP
            both = acc[at : at + GROUP, :]
            at = at + COMP * PACK
            both = both + acc[at : at + GROUP, :]
            mixed = None
            for o in range(1, n_inst):
                term = weights[o - 1] * dirs[o, a, q]
                mixed = term if mixed is None else mixed + term
            if mixed is not None:
                both = mixed * vol[q] + both
            out_ref[a, q] = out_ref[a, q] + both

    for o in range(1, n_inst):
        inst_copy(o).wait_send()
    for c in to_up() + to_down():
        c.wait_send()

    @pl.when(r > 0)
    def _():
        for c in to_below():
            c.wait_send()

    @pl.when(r < n_row - 1)
    def _():
        for c in to_above():
            c.wait_send()

    arrived(LATE)
    boundary(LATE)
    acc[...] = product(boundary_place(LATE, 0), bounds)
    for q in range(blocks):
        for a in range(COMP):
            at = a * PACK + q * GROUP
            both = acc[at : at + GROUP, :]
            at = at + COMP * PACK
            out_ref[a, q] = out_ref[a, q] + (both + acc[at : at + GROUP, :])


def per_device(
    direction,
    time_matrix,
    volume,
    diag_jac,
    face_jac,
    face_left,
    face_right,
    bound_jac,
    bound_cell,
    send_cell,
):
    n_inst = lax.axis_size("inst")
    n_row = lax.axis_size("row")
    n_pitch = lax.axis_size("pitch")
    cells = direction.shape[2]
    faces = face_left.shape[0]
    bounds = bound_cell.shape[1]
    blocks = cells // (GROUP * LANE)
    f_tiles = faces // LANE
    b_tiles = bounds // LANE
    width = 2 * faces + 4 * bounds
    f32, i32, bf16 = jnp.float32, jnp.int32, jnp.bfloat16
    cell_view = (blocks, GROUP, LANE)
    bound_view = (b_tiles, 4, LANE)
    hbm = pl.BlockSpec(memory_space=pl.ANY)

    def by_tile(cell):
        return cell.reshape(4, b_tiles, LANE).transpose(1, 0, 2)

    index_rows = pl.cdiv(b_tiles * 4, blocks * GROUP)
    assert index_rows * blocks * GROUP == b_tiles * 4
    result = pl.pallas_call(
        functools.partial(kernel, n_inst, n_row, n_pitch),
        out_shape=pltpu.VMEM((COMP, *cell_view), f32),
        in_specs=[hbm] * 10,
        out_specs=pl.BlockSpec(memory_space=pltpu.VMEM),
        scratch_shapes=[
            pltpu.SMEM((n_inst, n_inst), f32),
            pltpu.VMEM((COMP, *cell_view), f32),
            pltpu.VMEM((cells,), f32),
            pltpu.VMEM(cell_view, f32),
            pltpu.VMEM((25, *cell_view), f32),
            pltpu.VMEM((50, f_tiles, LANE), f32),
            pltpu.VMEM((f_tiles, LANE), i32),
            pltpu.VMEM((f_tiles, LANE), i32),
            pltpu.VMEM((50, *bound_view), f32),
            pltpu.VMEM(bound_view, i32),
            pltpu.VMEM((n_inst, COMP, *cell_view), f32),
            pltpu.VMEM((4, COMP + index_rows, *cell_view), f32),
            pltpu.VMEM((4, *bound_view), i32),
            pltpu.VMEM((25, b_tiles, LANE), f32),
            pltpu.VMEM((COMP, *bound_view), f32),
            pltpu.VMEM((4, b_tiles, LANE), i32),
            pltpu.VMEM((TERMS, f_tiles, LANE), f32),
            pltpu.VMEM((4, TERMS, b_tiles, LANE), f32),
            pltpu.VMEM((TERMS * PACK, width), bf16),
            pltpu.VMEM((LANE, width), bf16),
            pltpu.VMEM((TERMS * PACK, LANE), f32),
            pltpu.SemaphoreType.DMA((1,)),
            pltpu.SemaphoreType.DMA((4,)),
            pltpu.SemaphoreType.REGULAR((3,)),
        ],
        compiler_params=pltpu.CompilerParams(collective_id=0, has_side_effects=True),
    )(
        time_matrix,
        direction[0].reshape(COMP, *cell_view),
        volume,
        diag_jac[0].reshape(25, *cell_view),
        face_jac[0].reshape(50, f_tiles, LANE),
        face_left.reshape(f_tiles, LANE),
        face_right.reshape(f_tiles, LANE),
        bound_jac[0].reshape(4, 50, b_tiles, LANE).transpose(1, 2, 0, 3),
        by_tile(bound_cell),
        by_tile(send_cell),
    )
    return result.reshape(1, COMP, cells)


def solution(mesh):
    return jax.shard_map(
        per_device,
        mesh=mesh,
        in_specs=(
            P("inst", None, ("row", "pitch")),
            P(),
            P(("row", "pitch")),
            P("inst", None, ("row", "pitch")),
            P("inst", None, ("row", "pitch")),
            P(("row", "pitch")),
            P(("row", "pitch")),
            P("inst", None, None, ("row", "pitch")),
            P(None, ("row", "pitch")),
            P(None, ("row", "pitch")),
        ),
        out_specs=P("inst", None, ("row", "pitch")),
        check_vma=False,
    )
```

```python
import functools
import jax
import jax.numpy as jnp
from jax import lax
from jax.experimental import pallas as pl
from jax.experimental.pallas import tpu as pltpu
from jax.sharding import PartitionSpec as P

LANE = 128
COMP = 5
TERMS = 2 * COMP
PACK = 16
GROUP = 4
MESH = pl.DeviceIdType.MESH


def gathered(own, cell):
    low = cell & (LANE - 1)
    high = cell >> 7
    chunks = own.shape[1] * GROUP
    masks = [high == h for h in range(chunks)]
    values = []
    for b in range(COMP):
        found = None
        for h in range(chunks):
            row = own[b, h // GROUP, pl.ds(h % GROUP, 1), :]
            part = jnp.take_along_axis(
                jnp.broadcast_to(row, cell.shape), low, axis=1, mode="promise_in_bounds"
            )
            found = part if h == 0 else jnp.where(masks[h], part, found)
        values.append(found)
    return values


def applied(block, base, values):
    result = []
    for a in range(COMP):
        total = None
        for b in range(COMP):
            term = block(base + COMP * a + b) * values[b]
            total = term if total is None else total + term
        result.append(total)
    return result


def two_terms(value):
    first = value.astype(jnp.bfloat16).astype(jnp.float32)
    return first, value - first


def packed_row(row):
    return jnp.broadcast_to(row, (PACK, LANE)).astype(jnp.bfloat16)


def hot_tile(hot, place, cell_row, value):
    low = packed_row((cell_row & (LANE - 1)).astype(jnp.float32))
    for s in range(0, LANE, PACK):
        index = lax.broadcasted_iota(jnp.int32, (PACK, LANE), 0) + s
        index = index.astype(jnp.float32).astype(jnp.bfloat16)
        hot[s : s + PACK, place : place + LANE] = jnp.where(
            index == low, jnp.bfloat16(value), jnp.bfloat16(0)
        )


def chunk_mask(cell_row):
    index = lax.broadcasted_iota(jnp.int32, (PACK, LANE), 0)
    index = index.astype(jnp.float32).astype(jnp.bfloat16)
    return index == packed_row((cell_row >> 7).astype(jnp.float32))


NEAR, LATE, BELOW, ABOVE = 0, 1, 2, 3


def kernel(n_inst, n_row, n_pitch, *refs):
    pl.run_scoped(
        functools.partial(body, n_inst, n_row, n_pitch, *refs),
        pltpu.SemaphoreType.DMA((10,)),
        pltpu.SemaphoreType.DMA((n_inst + 8,)),
    )


def body(
    n_inst,
    n_row,
    n_pitch,
    tm_hbm,
    dir_hbm,
    vol_hbm,
    diag_hbm,
    face_hbm,
    left_hbm,
    right_hbm,
    bound_hbm,
    bcell_hbm,
    scell_hbm,
    out_ref,
    tm_ref,
    own,
    vol_line,
    vol,
    diag,
    face,
    left,
    right,
    bound,
    bcell,
    scell,
    dirs,
    ghost,
    ghost_cell,
    late_jac,
    inner_flux,
    place_cell,
    flux_terms,
    bound_terms,
    rows,
    hot,
    acc,
    inst_recv,
    ghost_recv,
    ready,
    local_sem,
    send_sem,
):
    t = lax.axis_index("inst")
    r = lax.axis_index("row")
    p = lax.axis_index("pitch")
    blocks = own.shape[1]
    chunks = blocks * GROUP
    f_tiles = left.shape[0]
    faces = f_tiles * LANE
    b_tiles = bcell.shape[0]
    bounds = b_tiles * LANE
    last = n_inst - 1

    barrier = pltpu.get_barrier_semaphore()

    def signal(sem, **place):
        pl.semaphore_signal(sem, inc=1, device_id=place, device_id_type=MESH)

    up = lax.rem(p + 1, n_pitch)
    down = lax.rem(p + n_pitch - 1, n_pitch)

    down_first = jnp.logical_and(p >= 1, jnp.logical_or(p < n_pitch - 1, t > 0))
    up_first = jnp.logical_or(
        p == n_pitch - 1, jnp.logical_and(p == n_pitch - 2, t == 0)
    )

    @pl.when(jnp.logical_not(down_first))
    def _():
        signal(barrier, pitch=down)

    @pl.when(jnp.logical_not(up_first))
    def _():
        signal(barrier, pitch=up)

    @pl.when(r < n_row - 1)
    def _():
        signal(barrier, row=r + 1)

    @pl.when(t == 0)
    def _():
        for u in range(1, n_inst):
            signal(barrier, inst=u)

    @pl.when(jnp.logical_and(t > 0, t < last))
    def _():
        signal(barrier, inst=last)

    pairs = [
        (dir_hbm, own),
        (bcell_hbm, bcell),
        (scell_hbm, scell),
        (left_hbm, left),
        (right_hbm, right),
        (face_hbm, face),
        (bound_hbm, bound),
        (diag_hbm, diag),
        (vol_hbm, vol_line),
        (tm_hbm, tm_ref),
    ]
    copies = [
        pltpu.make_async_copy(a, b, local_sem.at[i]) for i, (a, b) in enumerate(pairs)
    ]

    def ghost_copies(slot, at, early, **place):
        return [
            pltpu.make_async_remote_copy(
                src_ref=a,
                dst_ref=b,
                send_sem=send_sem.at[at + i],
                recv_sem=ghost_recv.at[slot],
                device_id=place,
                device_id_type=MESH,
            )
            for i, (a, b) in enumerate(
                [
                    (dir_hbm if early else own, ghost.at[slot, 0:COMP]),
                    (scell_hbm if early else scell, ghost_cell.at[slot]),
                ]
            )
        ]

    def to_up(early=False):
        slot = jnp.where(p == n_pitch - 1, LATE, NEAR)
        return ghost_copies(slot, n_inst, early, pitch=up)

    def to_down(early=False):
        slot = jnp.where(p == 1, NEAR, LATE)
        return ghost_copies(slot, n_inst + 2, early, pitch=down)

    def to_below():
        return ghost_copies(ABOVE, n_inst + 4, True, row=r - 1)

    def to_above():
        return ghost_copies(BELOW, n_inst + 6, False, row=r + 1)

    def start(group):
        for c in group:
            c.start()

    def inst_copy(o, early=False):
        return pltpu.make_async_remote_copy(
            src_ref=dir_hbm if early else own,
            dst_ref=dirs.at[o],
            send_sem=send_sem.at[o],
            recv_sem=inst_recv.at[0],
            device_id={"inst": lax.rem(t + o, n_inst)},
            device_id_type=MESH,
        )

    def inst_first(o):
        return jnp.logical_or(lax.rem(t + o, n_inst) == 0, t == last)

    greeted = jnp.where(t == last, last, jnp.where(t > 0, 1, 0))
    greeted = greeted + jnp.where(r > 0, 1, 0)
    greeted = greeted + jnp.where(down_first, 1, 0) + jnp.where(up_first, 1, 0)

    @pl.when(greeted > 0)
    def _():
        pl.semaphore_wait(barrier, greeted)

    @pl.when(up_first)
    def _():
        start(to_up(True))
        signal(ready.at[2], pitch=up)

    for o in range(1, n_inst):

        @pl.when(inst_first(o))
        def _(o=o):
            inst_copy(o, True).start()
            signal(ready.at[jnp.where(t == last, 3, 0)], inst=lax.rem(t + o, n_inst))

    @pl.when(down_first)
    def _():
        start(to_down(True))
        signal(ready.at[1], pitch=down)

    @pl.when(r > 0)
    def _():
        start(to_below())
        signal(ready.at[0], row=r - 1)

    start(copies)

    @pl.when(r == 0)
    def _():
        ghost[BELOW] = jnp.zeros(ghost.shape[1:], jnp.float32)
        ghost_cell[BELOW] = jnp.zeros(ghost_cell.shape[1:], jnp.int32)

    @pl.when(r == n_row - 1)
    def _():
        ghost[ABOVE] = jnp.zeros(ghost.shape[1:], jnp.float32)
        ghost_cell[ABOVE] = jnp.zeros(ghost_cell.shape[1:], jnp.int32)

    for c in copies:
        c.wait()

    def product(start, size):
        return lax.dot_general(
            rows[:, start : start + size],
            hot[:, start : start + size],
            (((1,), (1,)), ((), ())),
            preferred_element_type=jnp.float32,
        )

    total = None
    for g in range(0, f_tiles, 8):
        block = lambda i, g=g: face[i, g : g + 8, :]
        cell_l = left[g : g + 8, :]
        cell_r = right[g : g + 8, :]
        one = applied(block, 0, gathered(own, cell_l))
        two = applied(block, COMP * COMP, gathered(own, cell_r))
        for a in range(COMP):
            first, rest = two_terms(one[a] + two[a])
            flux_terms[a, g : g + 8, :] = first
            flux_terms[COMP + a, g : g + 8, :] = rest
        for s in range(g, g + 8):
            place = 2 * s * LANE
            row_l = left[s : s + 1, :]
            row_r = right[s : s + 1, :]
            hot_tile(hot, place, row_l, 1.0)
            hot_tile(hot, place + LANE, row_r, -1.0)
            mask_l = chunk_mask(row_l)
            mask_r = chunk_mask(row_r)
            for a in range(TERMS):
                value = packed_row(flux_terms[a, s : s + 1, :])
                at = slice(a * PACK, (a + 1) * PACK)
                zero = jnp.bfloat16(0)
                rows[at, place : place + LANE] = jnp.where(mask_l, value, zero)
                rows[at, place + LANE : place + 2 * LANE] = jnp.where(mask_r, value, zero)
        part = product(2 * g * LANE, 16 * LANE)
        total = part if total is None else total + part
    acc[...] = total

    edge = p == 0

    def side(slot, pick):
        if slot >= BELOW:
            return pick(slot)
        if slot == NEAR:
            return jnp.where(edge, pick(1), pick(0))
        return jnp.where(edge, pick(0), pick(1))

    def boundary_place(slot, j):
        return 2 * faces + ((3 - slot) * b_tiles + j) * LANE

    for j in range(b_tiles):
        block = lambda i, j=j: bound[i, j]
        flux = applied(block, 0, gathered(own, bcell[j]))
        for a in range(COMP):
            inner_flux[a, j] = flux[a]
    for slot in range(4):
        place_cell[slot] = side(slot, lambda k: bcell[:, k, :])
        for j in range(b_tiles):
            hot_tile(hot, boundary_place(slot, j), place_cell[slot, j : j + 1, :], 1.0)
    for i in range(COMP * COMP):
        late_jac[i] = side(LATE, lambda k, i=i: bound[COMP * COMP + i, :, k, :])

    for h in range(chunks):
        vol[h // GROUP, pl.ds(h % GROUP, 1), :] = vol_line[
            h * LANE : (h + 1) * LANE
        ].reshape(1, LANE)

    for q in range(blocks):
        local = applied(lambda i, q=q: diag[i, q], 0, [own[b, q] for b in range(COMP)])
        for a in range(COMP):
            out_ref[a, q] = local[a] + (tm_ref[t, t] * own[a, q]) * vol[q]

    answered = jnp.where(t == 0, max(n_inst - 2, 0), 0)
    answered = answered + jnp.where(r < n_row - 1, 1, 0)

    @pl.when(answered > 0)
    def _():
        pl.semaphore_wait(ready.at[0], answered)

    @pl.when(t == 0)
    def _():
        for o in range(1, last):
            inst_copy(o).start()

    @pl.when(r < n_row - 1)
    def _():
        start(to_above())

    @pl.when(jnp.logical_not(up_first))
    def _():
        pl.semaphore_wait(ready.at[1], 1)
        start(to_up())

    def answer_down():
        pl.semaphore_wait(ready.at[2], 1)
        start(to_down())

    @pl.when(jnp.logical_and(p > 0, jnp.logical_not(down_first)))
    def _():
        answer_down()

    @pl.when(t < last)
    def _():
        pl.semaphore_wait(ready.at[3], 1)
        for o in range(1, n_inst):
            u = lax.rem(t + o, n_inst)

            @pl.when(jnp.logical_or(u == last, jnp.logical_and(t > 0, u > 0)))
            def _(o=o):
                inst_copy(o).start()

    @pl.when(p == 0)
    def _():
        answer_down()

    def arrived(slot):
        pltpu.make_async_copy(ghost.at[slot], ghost.at[slot], ghost_recv.at[slot]).wait()

    def boundary(slot):
        cell = side(slot, lambda k: ghost_cell[slot, :, k ^ 1, :])
        values = gathered(ghost.at[slot], cell)
        if slot == LATE:
            block = lambda i: late_jac[i - COMP * COMP]
        else:
            block = lambda i: side(slot, lambda k: bound[i, :, k, :])
        flux = applied(block, COMP * COMP, values)
        for a in range(COMP):
            inner = side(slot, lambda k, a=a: inner_flux[a, :, k, :])
            first, rest = two_terms(inner + flux[a])
            bound_terms[slot, a] = first
            bound_terms[slot, COMP + a] = rest
        for j in range(b_tiles):
            place = boundary_place(slot, j)
            mask = chunk_mask(place_cell[slot, j : j + 1, :])
            for a in range(TERMS):
                value = packed_row(bound_terms[slot, a, j : j + 1, :])
                rows[a * PACK : (a + 1) * PACK, place : place + LANE] = jnp.where(
                    mask, value, jnp.bfloat16(0)
                )

    @pl.when(r > 0)
    def _():
        arrived(BELOW)

    @pl.when(r < n_row - 1)
    def _():
        arrived(ABOVE)

    boundary(ABOVE)
    boundary(BELOW)
    acc[...] = acc[...] + product(2 * faces, 2 * bounds)

    arrived(NEAR)
    boundary(NEAR)
    acc[...] = acc[...] + product(boundary_place(NEAR, 0), bounds)

    @pl.when(p > 0)
    def _():
        arrived(LATE)
        boundary(LATE)
        acc[...] = acc[...] + product(boundary_place(LATE, 0), bounds)

    if n_inst > 1:
        others = dirs.at[1:n_inst]
        pltpu.make_async_copy(others, others, inst_recv.at[0]).wait()
    weights = [tm_ref[t, lax.rem(t + n_inst - o, n_inst)] for o in range(1, n_inst)]
    for q in range(blocks):
        for a in range(COMP):
            at = a * PACK + q * GROUP
            both = acc[at : at + GROUP, :]
            at = at + COMP * PACK
            both = both + acc[at : at + GROUP, :]
            mixed = None
            for o in range(1, n_inst):
                term = weights[o - 1] * dirs[o, a, q]
                mixed = term if mixed is None else mixed + term
            if mixed is not None:
                both = mixed * vol[q] + both
            out_ref[a, q] = out_ref[a, q] + both

    @pl.when(p == 0)
    def _():
        arrived(LATE)
        boundary(LATE)
        acc[...] = product(boundary_place(LATE, 0), bounds)
        for q in range(blocks):
            for a in range(COMP):
                at = a * PACK + q * GROUP
                both = acc[at : at + GROUP, :]
                at = at + COMP * PACK
                out_ref[a, q] = out_ref[a, q] + (both + acc[at : at + GROUP, :])

    for o in range(1, n_inst):
        inst_copy(o).wait_send()
    for c in to_up() + to_down():
        c.wait_send()

    @pl.when(r > 0)
    def _():
        for c in to_below():
            c.wait_send()

    @pl.when(r < n_row - 1)
    def _():
        for c in to_above():
            c.wait_send()


def per_device(
    direction,
    time_matrix,
    volume,
    diag_jac,
    face_jac,
    face_left,
    face_right,
    bound_jac,
    bound_cell,
    send_cell,
):
    n_inst = lax.axis_size("inst")
    n_row = lax.axis_size("row")
    n_pitch = lax.axis_size("pitch")
    cells = direction.shape[2]
    faces = face_left.shape[0]
    bounds = bound_cell.shape[1]
    blocks = cells // (GROUP * LANE)
    f_tiles = faces // LANE
    b_tiles = bounds // LANE
    width = 2 * faces + 4 * bounds
    f32, i32, bf16 = jnp.float32, jnp.int32, jnp.bfloat16
    cell_view = (blocks, GROUP, LANE)
    bound_view = (b_tiles, 4, LANE)
    hbm = pl.BlockSpec(memory_space=pl.ANY)

    def by_tile(cell):
        return cell.reshape(4, b_tiles, LANE).transpose(1, 0, 2)

    index_rows = pl.cdiv(b_tiles * 4, blocks * GROUP)
    assert index_rows * blocks * GROUP == b_tiles * 4
    result = pl.pallas_call(
        functools.partial(kernel, n_inst, n_row, n_pitch),
        out_shape=pltpu.VMEM((COMP, *cell_view), f32),
        in_specs=[hbm] * 10,
        out_specs=pl.BlockSpec(memory_space=pltpu.VMEM),
        scratch_shapes=[
            pltpu.SMEM((n_inst, n_inst), f32),
            pltpu.VMEM((COMP, *cell_view), f32),
            pltpu.VMEM((cells,), f32),
            pltpu.VMEM(cell_view, f32),
            pltpu.VMEM((25, *cell_view), f32),
            pltpu.VMEM((50, f_tiles, LANE), f32),
            pltpu.VMEM((f_tiles, LANE), i32),
            pltpu.VMEM((f_tiles, LANE), i32),
            pltpu.VMEM((50, *bound_view), f32),
            pltpu.VMEM(bound_view, i32),
            pltpu.VMEM(bound_view, i32),
            pltpu.VMEM((n_inst, COMP, *cell_view), f32),
            pltpu.VMEM((4, COMP + index_rows, *cell_view), f32),
            pltpu.VMEM((4, *bound_view), i32),
            pltpu.VMEM((25, b_tiles, LANE), f32),
            pltpu.VMEM((COMP, *bound_view), f32),
            pltpu.VMEM((4, b_tiles, LANE), i32),
            pltpu.VMEM((TERMS, f_tiles, LANE), f32),
            pltpu.VMEM((4, TERMS, b_tiles, LANE), f32),
            pltpu.VMEM((TERMS * PACK, width), bf16),
            pltpu.VMEM((LANE, width), bf16),
            pltpu.VMEM((TERMS * PACK, LANE), f32),
            pltpu.SemaphoreType.DMA((1,)),
            pltpu.SemaphoreType.DMA((4,)),
            pltpu.SemaphoreType.REGULAR((4,)),
        ],
        compiler_params=pltpu.CompilerParams(collective_id=0, has_side_effects=True),
    )(
        time_matrix,
        direction[0].reshape(COMP, *cell_view),
        volume,
        diag_jac[0].reshape(25, *cell_view),
        face_jac[0].reshape(50, f_tiles, LANE),
        face_left.reshape(f_tiles, LANE),
        face_right.reshape(f_tiles, LANE),
        bound_jac[0].reshape(4, 50, b_tiles, LANE).transpose(1, 2, 0, 3),
        by_tile(bound_cell),
        by_tile(send_cell),
    )
    return result.reshape(1, COMP, cells)


def solution(mesh):
    return jax.shard_map(
        per_device,
        mesh=mesh,
        in_specs=(
            P("inst", None, ("row", "pitch")),
            P(),
            P(("row", "pitch")),
            P("inst", None, ("row", "pitch")),
            P("inst", None, ("row", "pitch")),
            P(("row", "pitch")),
            P(("row", "pitch")),
            P("inst", None, None, ("row", "pitch")),
            P(None, ("row", "pitch")),
            P(None, ("row", "pitch")),
        ),
        out_specs=P("inst", None, ("row", "pitch")),
        check_vma=False,
    )
```

```python
import functools
import jax
import jax.numpy as jnp
from jax import lax
from jax.experimental import pallas as pl
from jax.experimental.pallas import tpu as pltpu
from jax.sharding import PartitionSpec as P

LANE = 128
COMP = 5
TERMS = 2 * COMP
PACK = 16
GROUP = 4
MESH = pl.DeviceIdType.MESH


def gathered(own, cell):
    low = cell & (LANE - 1)
    high = cell >> 7
    chunks = own.shape[1] * GROUP
    masks = [high == h for h in range(chunks)]
    values = []
    for b in range(COMP):
        found = None
        for h in range(chunks):
            row = own[b, h // GROUP, pl.ds(h % GROUP, 1), :]
            part = jnp.take_along_axis(
                jnp.broadcast_to(row, cell.shape), low, axis=1, mode="promise_in_bounds"
            )
            found = part if h == 0 else jnp.where(masks[h], part, found)
        values.append(found)
    return values


def applied(block, base, values):
    result = []
    for a in range(COMP):
        total = None
        for b in range(COMP):
            term = block(base + COMP * a + b) * values[b]
            total = term if total is None else total + term
        result.append(total)
    return result


def two_terms(value):
    first = value.astype(jnp.bfloat16).astype(jnp.float32)
    return first, value - first


def packed_row(row):
    return jnp.broadcast_to(row, (PACK, LANE)).astype(jnp.bfloat16)


def hot_tile(hot, place, cell_row, value):
    low = packed_row((cell_row & (LANE - 1)).astype(jnp.float32))
    for s in range(0, LANE, PACK):
        index = lax.broadcasted_iota(jnp.int32, (PACK, LANE), 0) + s
        index = index.astype(jnp.float32).astype(jnp.bfloat16)
        hot[s : s + PACK, place : place + LANE] = jnp.where(
            index == low, jnp.bfloat16(value), jnp.bfloat16(0)
        )


def chunk_mask(cell_row):
    index = lax.broadcasted_iota(jnp.int32, (PACK, LANE), 0)
    index = index.astype(jnp.float32).astype(jnp.bfloat16)
    return index == packed_row((cell_row >> 7).astype(jnp.float32))


NEAR, LATE, BELOW, ABOVE = 0, 1, 2, 3
ORDER = (2, 3, 1, 0)


def kernel(n_inst, n_row, n_pitch, *refs):
    pl.run_scoped(
        functools.partial(body, n_inst, n_row, n_pitch, *refs),
        pltpu.SemaphoreType.DMA((10,)),
        pltpu.SemaphoreType.DMA((n_inst + 8,)),
    )


def body(
    n_inst,
    n_row,
    n_pitch,
    tm_hbm,
    dir_hbm,
    vol_hbm,
    diag_hbm,
    face_hbm,
    left_hbm,
    right_hbm,
    bound_hbm,
    bcell_hbm,
    scell_hbm,
    out_ref,
    tm_ref,
    own,
    vol_line,
    vol,
    diag,
    face,
    left,
    right,
    bound,
    bcell,
    scell,
    dirs,
    ghost,
    ghost_cell,
    late_jac,
    inner_flux,
    place_cell,
    flux_terms,
    bound_terms,
    rows,
    hot,
    acc,
    inst_recv,
    ghost_recv,
    ready,
    local_sem,
    send_sem,
):
    t = lax.axis_index("inst")
    r = lax.axis_index("row")
    p = lax.axis_index("pitch")
    blocks = own.shape[1]
    chunks = blocks * GROUP
    f_tiles = left.shape[0]
    faces = f_tiles * LANE
    b_tiles = bcell.shape[0]
    bounds = b_tiles * LANE
    last = n_inst - 1

    barrier = pltpu.get_barrier_semaphore()

    def signal(sem, **place):
        pl.semaphore_signal(sem, inc=1, device_id=place, device_id_type=MESH)

    up = lax.rem(p + 1, n_pitch)
    down = lax.rem(p + n_pitch - 1, n_pitch)

    down_first = jnp.logical_and(p >= 1, jnp.logical_or(p < n_pitch - 1, t > 0))
    up_first = jnp.logical_or(
        p == n_pitch - 1, jnp.logical_and(p == n_pitch - 2, t == 0)
    )

    @pl.when(jnp.logical_not(down_first))
    def _():
        signal(barrier, pitch=down)

    @pl.when(jnp.logical_not(up_first))
    def _():
        signal(barrier, pitch=up)

    @pl.when(r < n_row - 1)
    def _():
        signal(barrier, row=r + 1)

    @pl.when(t == 0)
    def _():
        for u in range(1, n_inst):
            signal(barrier, inst=u)

    @pl.when(jnp.logical_and(t > 0, t < last))
    def _():
        signal(barrier, inst=last)

    pairs = [
        (dir_hbm, own),
        (bcell_hbm, bcell),
        (scell_hbm, scell),
        (left_hbm, left),
        (right_hbm, right),
        (face_hbm, face),
        (bound_hbm, bound),
        (diag_hbm, diag),
        (vol_hbm, vol_line),
        (tm_hbm, tm_ref),
    ]
    copies = [
        pltpu.make_async_copy(a, b, local_sem.at[i]) for i, (a, b) in enumerate(pairs)
    ]

    def ghost_copies(slot, at, early, **place):
        return [
            pltpu.make_async_remote_copy(
                src_ref=a,
                dst_ref=b,
                send_sem=send_sem.at[at + i],
                recv_sem=ghost_recv.at[slot],
                device_id=place,
                device_id_type=MESH,
            )
            for i, (a, b) in enumerate(
                [
                    (dir_hbm if early else own, ghost.at[slot, 0:COMP]),
                    (scell_hbm if early else scell, ghost_cell.at[slot]),
                ]
            )
        ]

    def to_up(early=False):
        slot = jnp.where(p == n_pitch - 1, LATE, NEAR)
        return ghost_copies(slot, n_inst, early, pitch=up)

    def to_down():
        slot = jnp.where(p == 1, NEAR, LATE)
        return ghost_copies(slot, n_inst + 2, False, pitch=down)

    def to_below():
        return ghost_copies(ABOVE, n_inst + 4, True, row=r - 1)

    def to_above():
        return ghost_copies(BELOW, n_inst + 6, False, row=r + 1)

    def start(group):
        for c in group:
            c.start()

    def inst_copy(o, early=False):
        return pltpu.make_async_remote_copy(
            src_ref=dir_hbm if early else own,
            dst_ref=dirs.at[o],
            send_sem=send_sem.at[o],
            recv_sem=inst_recv.at[0],
            device_id={"inst": lax.rem(t + o, n_inst)},
            device_id_type=MESH,
        )

    def inst_first(o):
        return jnp.logical_or(lax.rem(t + o, n_inst) == 0, t == last)

    greeted = jnp.where(t == last, last, jnp.where(t > 0, 1, 0))
    greeted = greeted + jnp.where(r > 0, 1, 0)
    greeted = greeted + jnp.where(down_first, 1, 0) + jnp.where(up_first, 1, 0)

    @pl.when(greeted > 0)
    def _():
        pl.semaphore_wait(barrier, greeted)

    leads = jnp.logical_and(p == n_pitch - 1, r == 0)

    @pl.when(up_first)
    def _():
        signal(ready.at[1], pitch=up)

    @pl.when(leads)
    def _():
        start(to_up(True))

    for o in range(1, n_inst):

        @pl.when(inst_first(o))
        def _(o=o):
            inst_copy(o, True).start()
            signal(ready.at[jnp.where(t == last, 2, 0)], inst=lax.rem(t + o, n_inst))

    @pl.when(down_first)
    def _():
        signal(ready.at[0], pitch=down)

    @pl.when(r > 0)
    def _():
        start(to_below())
        signal(ready.at[0], row=r - 1)

    start(copies)

    @pl.when(r == 0)
    def _():
        ghost[BELOW] = jnp.zeros(ghost.shape[1:], jnp.float32)
        ghost_cell[BELOW] = jnp.zeros(ghost_cell.shape[1:], jnp.int32)

    @pl.when(r == n_row - 1)
    def _():
        ghost[ABOVE] = jnp.zeros(ghost.shape[1:], jnp.float32)
        ghost_cell[ABOVE] = jnp.zeros(ghost_cell.shape[1:], jnp.int32)

    for c in copies[0:3]:
        c.wait()

    @pl.when(jnp.logical_and(up_first, jnp.logical_not(leads)))
    def _():
        start(to_up())

    @pl.when(down_first)
    def _():
        start(to_down())

    for c in copies[3:]:
        c.wait()

    def product(start, size):
        return lax.dot_general(
            rows[:, start : start + size],
            hot[:, start : start + size],
            (((1,), (1,)), ((), ())),
            preferred_element_type=jnp.float32,
        )

    total = None
    for g in range(0, f_tiles, 8):
        block = lambda i, g=g: face[i, g : g + 8, :]
        cell_l = left[g : g + 8, :]
        cell_r = right[g : g + 8, :]
        one = applied(block, 0, gathered(own, cell_l))
        two = applied(block, COMP * COMP, gathered(own, cell_r))
        for a in range(COMP):
            first, rest = two_terms(one[a] + two[a])
            flux_terms[a, g : g + 8, :] = first
            flux_terms[COMP + a, g : g + 8, :] = rest
        for s in range(g, g + 8):
            place = 2 * s * LANE
            row_l = left[s : s + 1, :]
            row_r = right[s : s + 1, :]
            hot_tile(hot, place, row_l, 1.0)
            hot_tile(hot, place + LANE, row_r, -1.0)
            mask_l = chunk_mask(row_l)
            mask_r = chunk_mask(row_r)
            for a in range(TERMS):
                value = packed_row(flux_terms[a, s : s + 1, :])
                at = slice(a * PACK, (a + 1) * PACK)
                zero = jnp.bfloat16(0)
                rows[at, place : place + LANE] = jnp.where(mask_l, value, zero)
                rows[at, place + LANE : place + 2 * LANE] = jnp.where(mask_r, value, zero)
        part = product(2 * g * LANE, 16 * LANE)
        total = part if total is None else total + part
    acc[...] = total

    edge = p == 0

    def side(slot, pick):
        if slot >= BELOW:
            return pick(slot)
        if slot == NEAR:
            return jnp.where(edge, pick(1), pick(0))
        return jnp.where(edge, pick(0), pick(1))

    def boundary_place(slot, j):
        return 2 * faces + (ORDER[slot] * b_tiles + j) * LANE

    for j in range(b_tiles):
        block = lambda i, j=j: bound[i, j]
        flux = applied(block, 0, gathered(own, bcell[j]))
        for a in range(COMP):
            inner_flux[a, j] = flux[a]
    for slot in range(4):
        place_cell[slot] = side(slot, lambda k: bcell[:, k, :])
        for j in range(b_tiles):
            place = boundary_place(slot, j)
            hot_tile(hot, place, place_cell[slot, j : j + 1, :], 1.0)
            if slot == LATE:
                hot[:, place + bounds : place + bounds + LANE] = hot[:, place : place + LANE]
    for i in range(COMP * COMP):
        late_jac[i] = side(LATE, lambda k, i=i: bound[COMP * COMP + i, :, k, :])

    for h in range(chunks):
        vol[h // GROUP, pl.ds(h % GROUP, 1), :] = vol_line[
            h * LANE : (h + 1) * LANE
        ].reshape(1, LANE)

    for q in range(blocks):
        local = applied(lambda i, q=q: diag[i, q], 0, [own[b, q] for b in range(COMP)])
        for a in range(COMP):
            out_ref[a, q] = local[a] + (tm_ref[t, t] * own[a, q]) * vol[q]

    answered = jnp.where(t == 0, max(n_inst - 2, 0), 0)
    answered = answered + jnp.where(r < n_row - 1, 1, 0)
    answered = answered + jnp.where(up_first, 0, 1)

    @pl.when(answered > 0)
    def _():
        pl.semaphore_wait(ready.at[0], answered)

    @pl.when(t == 0)
    def _():
        for o in range(1, last):
            inst_copy(o).start()

    @pl.when(r < n_row - 1)
    def _():
        start(to_above())

    @pl.when(jnp.logical_not(up_first))
    def _():
        start(to_up())

    def answer_down():
        pl.semaphore_wait(ready.at[1], 1)
        start(to_down())

    @pl.when(jnp.logical_and(p > 0, jnp.logical_not(down_first)))
    def _():
        answer_down()

    @pl.when(t < last)
    def _():
        pl.semaphore_wait(ready.at[2], 1)
        for o in range(1, n_inst):
            u = lax.rem(t + o, n_inst)

            @pl.when(jnp.logical_or(u == last, jnp.logical_and(t > 0, u > 0)))
            def _(o=o):
                inst_copy(o).start()

    @pl.when(p == 0)
    def _():
        answer_down()

    def arrived(slot):
        pltpu.make_async_copy(ghost.at[slot], ghost.at[slot], ghost_recv.at[slot]).wait()

    def boundary(slot):
        cell = side(slot, lambda k: ghost_cell[slot, :, k ^ 1, :])
        total = [side(slot, lambda k, a=a: inner_flux[a, :, k, :]) for a in range(COMP)]
        for b, value in enumerate(gathered(ghost.at[slot], cell)):
            for a in range(COMP):
                i = COMP * a + b
                if slot == LATE:
                    block = late_jac[i]
                else:
                    block = side(slot, lambda k: bound[COMP * COMP + i, :, k, :])
                total[a] = total[a] + block * value
        for a in range(COMP):
            first, rest = two_terms(total[a])
            bound_terms[slot, a] = first
            bound_terms[slot, COMP + a] = rest
        for j in range(b_tiles):
            mask = chunk_mask(place_cell[slot, j : j + 1, :])
            for a in range(TERMS):
                value = packed_row(bound_terms[slot, a, j : j + 1, :])
                term, place = a, boundary_place(slot, j)
                if slot == LATE and a >= COMP:
                    term, place = a - COMP, place + bounds
                rows[term * PACK : (term + 1) * PACK, place : place + LANE] = jnp.where(
                    mask, value, jnp.bfloat16(0)
                )

    def late_product():
        at = slice(boundary_place(LATE, 0), boundary_place(LATE, 0) + 2 * bounds)
        return lax.dot_general(
            rows[0 : COMP * PACK, at],
            hot[:, at],
            (((1,), (1,)), ((), ())),
            preferred_element_type=jnp.float32,
        )

    @pl.when(r > 0)
    def _():
        arrived(BELOW)

    @pl.when(r < n_row - 1)
    def _():
        arrived(ABOVE)

    boundary(ABOVE)
    boundary(BELOW)
    acc[...] = acc[...] + product(2 * faces, 2 * bounds)

    arrived(NEAR)
    boundary(NEAR)
    acc[...] = acc[...] + product(boundary_place(NEAR, 0), bounds)

    @pl.when(p > 0)
    def _():
        arrived(LATE)
        boundary(LATE)
        acc[0 : COMP * PACK] = acc[0 : COMP * PACK] + late_product()

    if n_inst > 1:
        others = dirs.at[1:n_inst]
        pltpu.make_async_copy(others, others, inst_recv.at[0]).wait()
    weights = [tm_ref[t, lax.rem(t + n_inst - o, n_inst)] for o in range(1, n_inst)]
    for q in range(blocks):
        for a in range(COMP):
            at = a * PACK + q * GROUP
            both = acc[at : at + GROUP, :]
            at = at + COMP * PACK
            both = both + acc[at : at + GROUP, :]
            mixed = None
            for o in range(1, n_inst):
                term = weights[o - 1] * dirs[o, a, q]
                mixed = term if mixed is None else mixed + term
            if mixed is not None:
                both = mixed * vol[q] + both
            out_ref[a, q] = out_ref[a, q] + both

    @pl.when(p == 0)
    def _():
        arrived(LATE)
        boundary(LATE)
        acc[0 : COMP * PACK] = late_product()
        for q in range(blocks):
            for a in range(COMP):
                at = a * PACK + q * GROUP
                out_ref[a, q] = out_ref[a, q] + acc[at : at + GROUP, :]

    for o in range(1, n_inst):
        inst_copy(o).wait_send()
    for c in to_up() + to_down():
        c.wait_send()

    @pl.when(r > 0)
    def _():
        for c in to_below():
            c.wait_send()

    @pl.when(r < n_row - 1)
    def _():
        for c in to_above():
            c.wait_send()


def per_device(
    direction,
    time_matrix,
    volume,
    diag_jac,
    face_jac,
    face_left,
    face_right,
    bound_jac,
    bound_cell,
    send_cell,
):
    n_inst = lax.axis_size("inst")
    n_row = lax.axis_size("row")
    n_pitch = lax.axis_size("pitch")
    cells = direction.shape[2]
    faces = face_left.shape[0]
    bounds = bound_cell.shape[1]
    blocks = cells // (GROUP * LANE)
    f_tiles = faces // LANE
    b_tiles = bounds // LANE
    width = 2 * faces + 5 * bounds
    f32, i32, bf16 = jnp.float32, jnp.int32, jnp.bfloat16
    cell_view = (blocks, GROUP, LANE)
    bound_view = (b_tiles, 4, LANE)
    hbm = pl.BlockSpec(memory_space=pl.ANY)

    def by_tile(cell):
        return cell.reshape(4, b_tiles, LANE).transpose(1, 0, 2)

    index_rows = pl.cdiv(b_tiles * 4, blocks * GROUP)
    assert index_rows * blocks * GROUP == b_tiles * 4
    result = pl.pallas_call(
        functools.partial(kernel, n_inst, n_row, n_pitch),
        out_shape=pltpu.VMEM((COMP, *cell_view), f32),
        in_specs=[hbm] * 10,
        out_specs=pl.BlockSpec(memory_space=pltpu.VMEM),
        scratch_shapes=[
            pltpu.SMEM((n_inst, n_inst), f32),
            pltpu.VMEM((COMP, *cell_view), f32),
            pltpu.VMEM((cells,), f32),
            pltpu.VMEM(cell_view, f32),
            pltpu.VMEM((25, *cell_view), f32),
            pltpu.VMEM((50, f_tiles, LANE), f32),
            pltpu.VMEM((f_tiles, LANE), i32),
            pltpu.VMEM((f_tiles, LANE), i32),
            pltpu.VMEM((50, *bound_view), f32),
            pltpu.VMEM(bound_view, i32),
            pltpu.VMEM(bound_view, i32),
            pltpu.VMEM((n_inst, COMP, *cell_view), f32),
            pltpu.VMEM((4, COMP + index_rows, *cell_view), f32),
            pltpu.VMEM((4, *bound_view), i32),
            pltpu.VMEM((25, b_tiles, LANE), f32),
            pltpu.VMEM((COMP, *bound_view), f32),
            pltpu.VMEM((4, b_tiles, LANE), i32),
            pltpu.VMEM((TERMS, f_tiles, LANE), f32),
            pltpu.VMEM((4, TERMS, b_tiles, LANE), f32),
            pltpu.VMEM((TERMS * PACK, width), bf16),
            pltpu.VMEM((LANE, width), bf16),
            pltpu.VMEM((TERMS * PACK, LANE), f32),
            pltpu.SemaphoreType.DMA((1,)),
            pltpu.SemaphoreType.DMA((4,)),
            pltpu.SemaphoreType.REGULAR((3,)),
        ],
        compiler_params=pltpu.CompilerParams(collective_id=0, has_side_effects=True),
    )(
        time_matrix,
        direction[0].reshape(COMP, *cell_view),
        volume,
        diag_jac[0].reshape(25, *cell_view),
        face_jac[0].reshape(50, f_tiles, LANE),
        face_left.reshape(f_tiles, LANE),
        face_right.reshape(f_tiles, LANE),
        bound_jac[0].reshape(4, 50, b_tiles, LANE).transpose(1, 2, 0, 3),
        by_tile(bound_cell),
        by_tile(send_cell),
    )
    return result.reshape(1, COMP, cells)


def solution(mesh):
    return jax.shard_map(
        per_device,
        mesh=mesh,
        in_specs=(
            P("inst", None, ("row", "pitch")),
            P(),
            P(("row", "pitch")),
            P("inst", None, ("row", "pitch")),
            P("inst", None, ("row", "pitch")),
            P(("row", "pitch")),
            P(("row", "pitch")),
            P("inst", None, None, ("row", "pitch")),
            P(None, ("row", "pitch")),
            P(None, ("row", "pitch")),
        ),
        out_specs=P("inst", None, ("row", "pitch")),
        check_vma=False,
    )
```

```python
import functools
import jax
import jax.numpy as jnp
from jax import lax
from jax.experimental import pallas as pl
from jax.experimental.pallas import tpu as pltpu
from jax.sharding import PartitionSpec as P

LANE = 128
COMP = 5
TERMS = 2 * COMP
PACK = 16
GROUP = 4
MESH = pl.DeviceIdType.MESH


def gathered(own, cell):
    low = cell & (LANE - 1)
    high = cell >> 7
    chunks = own.shape[1] * GROUP
    masks = [high == h for h in range(chunks)]
    values = []
    for b in range(COMP):
        found = None
        for h in range(chunks):
            row = own[b, h // GROUP, pl.ds(h % GROUP, 1), :]
            part = jnp.take_along_axis(
                jnp.broadcast_to(row, cell.shape), low, axis=1, mode="promise_in_bounds"
            )
            found = part if h == 0 else jnp.where(masks[h], part, found)
        values.append(found)
    return values


def applied(block, base, values):
    result = []
    for a in range(COMP):
        total = None
        for b in range(COMP):
            term = block(base + COMP * a + b) * values[b]
            total = term if total is None else total + term
        result.append(total)
    return result


def two_terms(value):
    first = value.astype(jnp.bfloat16).astype(jnp.float32)
    return first, value - first


def packed_row(row):
    return jnp.broadcast_to(row, (PACK, LANE)).astype(jnp.bfloat16)


def hot_tile(hot, place, cell_row, value):
    low = packed_row((cell_row & (LANE - 1)).astype(jnp.float32))
    for s in range(0, LANE, PACK):
        index = lax.broadcasted_iota(jnp.int32, (PACK, LANE), 0) + s
        index = index.astype(jnp.float32).astype(jnp.bfloat16)
        hot[s : s + PACK, place : place + LANE] = jnp.where(
            index == low, jnp.bfloat16(value), jnp.bfloat16(0)
        )


def chunk_mask(cell_row):
    index = lax.broadcasted_iota(jnp.int32, (PACK, LANE), 0)
    index = index.astype(jnp.float32).astype(jnp.bfloat16)
    return index == packed_row((cell_row >> 7).astype(jnp.float32))


NEAR, LATE, BELOW, ABOVE = 0, 1, 2, 3
ORDER = (2, 3, 1, 0)


def kernel(n_inst, n_row, n_pitch, *refs):
    pl.run_scoped(
        functools.partial(body, n_inst, n_row, n_pitch, *refs),
        pltpu.SemaphoreType.DMA((10,)),
        pltpu.SemaphoreType.DMA((n_inst + 8,)),
    )


def body(
    n_inst,
    n_row,
    n_pitch,
    tm_hbm,
    dir_hbm,
    vol_hbm,
    diag_hbm,
    face_hbm,
    left_hbm,
    right_hbm,
    bound_hbm,
    bcell_hbm,
    scell_hbm,
    out_ref,
    tm_ref,
    own,
    vol_line,
    vol,
    diag,
    face,
    left,
    right,
    bound,
    bcell,
    scell,
    dirs,
    ghost,
    ghost_cell,
    late_jac,
    late_hot,
    inner_flux,
    place_cell,
    flux_terms,
    bound_terms,
    rows,
    hot,
    acc,
    inst_recv,
    ghost_recv,
    ready,
    local_sem,
    send_sem,
):
    t = lax.axis_index("inst")
    r = lax.axis_index("row")
    p = lax.axis_index("pitch")
    blocks = own.shape[1]
    chunks = blocks * GROUP
    f_tiles = left.shape[0]
    faces = f_tiles * LANE
    b_tiles = bcell.shape[0]
    bounds = b_tiles * LANE
    last = n_inst - 1

    barrier = pltpu.get_barrier_semaphore()

    def signal(sem, **place):
        pl.semaphore_signal(sem, inc=1, device_id=place, device_id_type=MESH)

    up = lax.rem(p + 1, n_pitch)
    down = lax.rem(p + n_pitch - 1, n_pitch)

    down_first = jnp.logical_and(p >= 1, jnp.logical_or(p < n_pitch - 1, t > 0))
    up_first = jnp.logical_or(
        p == n_pitch - 1, jnp.logical_and(p == n_pitch - 2, t == 0)
    )

    @pl.when(jnp.logical_not(down_first))
    def _():
        signal(barrier, pitch=down)

    @pl.when(jnp.logical_not(up_first))
    def _():
        signal(barrier, pitch=up)

    pairs = [
        (dir_hbm, own),
        (bcell_hbm, bcell),
        (scell_hbm, scell),
        (left_hbm, left),
        (right_hbm, right),
        (face_hbm, face),
        (bound_hbm, bound),
        (diag_hbm, diag),
        (vol_hbm, vol_line),
        (tm_hbm, tm_ref),
    ]
    copies = [
        pltpu.make_async_copy(a, b, local_sem.at[i]) for i, (a, b) in enumerate(pairs)
    ]

    def ghost_copies(slot, at, early, **place):
        return [
            pltpu.make_async_remote_copy(
                src_ref=a,
                dst_ref=b,
                send_sem=send_sem.at[at + i],
                recv_sem=ghost_recv.at[slot],
                device_id=place,
                device_id_type=MESH,
            )
            for i, (a, b) in enumerate(
                [
                    (dir_hbm if early else own, ghost.at[slot, 0:COMP]),
                    (scell_hbm if early else scell, ghost_cell.at[slot]),
                ]
            )
        ]

    def to_up(early=False):
        slot = jnp.where(p == n_pitch - 1, LATE, NEAR)
        return ghost_copies(slot, n_inst, early, pitch=up)

    def to_down():
        slot = jnp.where(p == 1, NEAR, LATE)
        return ghost_copies(slot, n_inst + 2, False, pitch=down)

    def to_below():
        return ghost_copies(ABOVE, n_inst + 4, True, row=r - 1)

    def to_above():
        return ghost_copies(BELOW, n_inst + 6, False, row=r + 1)

    def start(group):
        for c in group:
            c.start()

    def inst_copy(o, early=False):
        return pltpu.make_async_remote_copy(
            src_ref=dir_hbm if early else own,
            dst_ref=dirs.at[o],
            send_sem=send_sem.at[o],
            recv_sem=inst_recv.at[0],
            device_id={"inst": lax.rem(t + o, n_inst)},
            device_id_type=MESH,
        )

    def inst_first(o):
        return jnp.logical_or(lax.rem(t + o, n_inst) == 0, t == last)

    leads = jnp.logical_and(p == n_pitch - 1, r == 0)
    first = jnp.logical_and(leads, t == 0)

    @pl.when(first)
    def _():
        pl.semaphore_wait(barrier, 1)
        start(to_up(True))

    @pl.when(r < n_row - 1)
    def _():
        signal(barrier, row=r + 1)

    @pl.when(t == 0)
    def _():
        for u in range(1, n_inst):
            signal(barrier, inst=u)

    @pl.when(jnp.logical_and(t > 0, t < last))
    def _():
        signal(barrier, inst=last)

    greeted = jnp.where(t == last, last, jnp.where(t > 0, 1, 0))
    greeted = greeted + jnp.where(r > 0, 1, 0)
    greeted = greeted + jnp.where(down_first, 1, 0) + jnp.where(up_first, 1, 0)

    @pl.when(jnp.logical_and(greeted > 0, jnp.logical_not(first)))
    def _():
        pl.semaphore_wait(barrier, greeted)

    @pl.when(up_first)
    def _():
        signal(ready.at[1], pitch=up)

    @pl.when(jnp.logical_and(leads, jnp.logical_not(first)))
    def _():
        start(to_up(True))

    for o in range(1, n_inst):

        @pl.when(inst_first(o))
        def _(o=o):
            inst_copy(o, True).start()
            signal(ready.at[jnp.where(t == last, 2, 0)], inst=lax.rem(t + o, n_inst))

    @pl.when(down_first)
    def _():
        signal(ready.at[0], pitch=down)

    @pl.when(r > 0)
    def _():
        start(to_below())
        signal(ready.at[0], row=r - 1)

    start(copies)

    @pl.when(r == 0)
    def _():
        ghost[BELOW] = jnp.zeros(ghost.shape[1:], jnp.float32)
        ghost_cell[BELOW] = jnp.zeros(ghost_cell.shape[1:], jnp.int32)

    @pl.when(r == n_row - 1)
    def _():
        ghost[ABOVE] = jnp.zeros(ghost.shape[1:], jnp.float32)
        ghost_cell[ABOVE] = jnp.zeros(ghost_cell.shape[1:], jnp.int32)

    for c in copies[0:3]:
        c.wait()

    @pl.when(jnp.logical_and(up_first, jnp.logical_not(leads)))
    def _():
        start(to_up())

    @pl.when(down_first)
    def _():
        start(to_down())

    for c in copies[3:]:
        c.wait()

    def product(start, size):
        return lax.dot_general(
            rows[:, start : start + size],
            hot[:, start : start + size],
            (((1,), (1,)), ((), ())),
            preferred_element_type=jnp.float32,
        )

    total = None
    for g in range(0, f_tiles, 8):
        block = lambda i, g=g: face[i, g : g + 8, :]
        cell_l = left[g : g + 8, :]
        cell_r = right[g : g + 8, :]
        one = applied(block, 0, gathered(own, cell_l))
        two = applied(block, COMP * COMP, gathered(own, cell_r))
        for a in range(COMP):
            first, rest = two_terms(one[a] + two[a])
            flux_terms[a, g : g + 8, :] = first
            flux_terms[COMP + a, g : g + 8, :] = rest
        for s in range(g, g + 8):
            place = 2 * s * LANE
            row_l = left[s : s + 1, :]
            row_r = right[s : s + 1, :]
            hot_tile(hot, place, row_l, 1.0)
            hot_tile(hot, place + LANE, row_r, -1.0)
            mask_l = chunk_mask(row_l)
            mask_r = chunk_mask(row_r)
            for a in range(TERMS):
                value = packed_row(flux_terms[a, s : s + 1, :])
                at = slice(a * PACK, (a + 1) * PACK)
                zero = jnp.bfloat16(0)
                rows[at, place : place + LANE] = jnp.where(mask_l, value, zero)
                rows[at, place + LANE : place + 2 * LANE] = jnp.where(mask_r, value, zero)
        part = product(2 * g * LANE, 16 * LANE)
        total = part if total is None else total + part
    acc[...] = total

    edge = p == 0

    def side(slot, pick):
        if slot >= BELOW:
            return pick(slot)
        if slot == NEAR:
            return jnp.where(edge, pick(1), pick(0))
        return jnp.where(edge, pick(0), pick(1))

    def boundary_place(slot, j):
        return 2 * faces + (ORDER[slot] * b_tiles + j) * LANE

    for j in range(b_tiles):
        block = lambda i, j=j: bound[i, j]
        flux = applied(block, 0, gathered(own, bcell[j]))
        for a in range(COMP):
            inner_flux[a, j] = flux[a]
    for slot in range(4):
        place_cell[slot] = side(slot, lambda k: bcell[:, k, :])
        for j in range(b_tiles):
            place = boundary_place(slot, j)
            hot_tile(hot, place, place_cell[slot, j : j + 1, :], 1.0)
            if slot == LATE:
                turned = hot[:, place : place + LANE].astype(jnp.float32).T
                turned = turned.astype(jnp.bfloat16)
                late_hot[j * LANE : (j + 1) * LANE, :] = turned
                late_hot[bounds + j * LANE : bounds + (j + 1) * LANE, :] = turned
    for i in range(COMP * COMP):
        late_jac[i] = side(LATE, lambda k, i=i: bound[COMP * COMP + i, :, k, :])

    for h in range(chunks):
        vol[h // GROUP, pl.ds(h % GROUP, 1), :] = vol_line[
            h * LANE : (h + 1) * LANE
        ].reshape(1, LANE)

    for q in range(blocks):
        local = applied(lambda i, q=q: diag[i, q], 0, [own[b, q] for b in range(COMP)])
        for a in range(COMP):
            out_ref[a, q] = local[a] + (tm_ref[t, t] * own[a, q]) * vol[q]

    answered = jnp.where(t == 0, max(n_inst - 2, 0), 0)
    answered = answered + jnp.where(r < n_row - 1, 1, 0)
    answered = answered + jnp.where(up_first, 0, 1)

    @pl.when(answered > 0)
    def _():
        pl.semaphore_wait(ready.at[0], answered)

    @pl.when(t == 0)
    def _():
        for o in range(1, last):
            inst_copy(o).start()

    @pl.when(r < n_row - 1)
    def _():
        start(to_above())

    @pl.when(jnp.logical_not(up_first))
    def _():
        start(to_up())

    def answer_down():
        pl.semaphore_wait(ready.at[1], 1)
        start(to_down())

    @pl.when(jnp.logical_and(p > 0, jnp.logical_not(down_first)))
    def _():
        answer_down()

    @pl.when(t < last)
    def _():
        pl.semaphore_wait(ready.at[2], 1)
        for o in range(1, n_inst):
            u = lax.rem(t + o, n_inst)

            @pl.when(jnp.logical_or(u == last, jnp.logical_and(t > 0, u > 0)))
            def _(o=o):
                inst_copy(o).start()

    @pl.when(p == 0)
    def _():
        answer_down()

    def arrived(slot):
        pltpu.make_async_copy(ghost.at[slot], ghost.at[slot], ghost_recv.at[slot]).wait()

    def boundary(slot):
        cell = side(slot, lambda k: ghost_cell[slot, :, k ^ 1, :])
        total = [side(slot, lambda k, a=a: inner_flux[a, :, k, :]) for a in range(COMP)]
        for b, value in enumerate(gathered(ghost.at[slot], cell)):
            for a in range(COMP):
                i = COMP * a + b
                if slot == LATE:
                    block = late_jac[i]
                else:
                    block = side(slot, lambda k: bound[COMP * COMP + i, :, k, :])
                total[a] = total[a] + block * value
        for a in range(COMP):
            first, rest = two_terms(total[a])
            bound_terms[slot, a] = first
            bound_terms[slot, COMP + a] = rest
        for j in range(b_tiles):
            mask = chunk_mask(place_cell[slot, j : j + 1, :])
            for a in range(TERMS):
                value = packed_row(bound_terms[slot, a, j : j + 1, :])
                term, place = a, boundary_place(slot, j)
                if slot == LATE and a >= COMP:
                    term, place = a - COMP, place + bounds
                rows[term * PACK : (term + 1) * PACK, place : place + LANE] = jnp.where(
                    mask, value, jnp.bfloat16(0)
                )

    def late_product():
        at = slice(boundary_place(LATE, 0), boundary_place(LATE, 0) + 2 * bounds)
        return lax.dot_general(
            rows[0 : COMP * PACK, at],
            late_hot[...],
            (((1,), (0,)), ((), ())),
            preferred_element_type=jnp.float32,
        )

    @pl.when(r > 0)
    def _():
        arrived(BELOW)

    @pl.when(r < n_row - 1)
    def _():
        arrived(ABOVE)

    boundary(ABOVE)
    boundary(BELOW)
    acc[...] = acc[...] + product(2 * faces, 2 * bounds)

    arrived(NEAR)
    boundary(NEAR)
    acc[...] = acc[...] + product(boundary_place(NEAR, 0), bounds)

    @pl.when(p > 0)
    def _():
        arrived(LATE)
        boundary(LATE)
        acc[0 : COMP * PACK] = acc[0 : COMP * PACK] + late_product()

    if n_inst > 1:
        others = dirs.at[1:n_inst]
        pltpu.make_async_copy(others, others, inst_recv.at[0]).wait()
    weights = [tm_ref[t, lax.rem(t + n_inst - o, n_inst)] for o in range(1, n_inst)]
    for q in range(blocks):
        for a in range(COMP):
            at = a * PACK + q * GROUP
            both = acc[at : at + GROUP, :]
            at = at + COMP * PACK
            both = both + acc[at : at + GROUP, :]
            mixed = None
            for o in range(1, n_inst):
                term = weights[o - 1] * dirs[o, a, q]
                mixed = term if mixed is None else mixed + term
            if mixed is not None:
                both = mixed * vol[q] + both
            out_ref[a, q] = out_ref[a, q] + both

    @pl.when(p == 0)
    def _():
        arrived(LATE)
        boundary(LATE)
        acc[0 : COMP * PACK] = late_product()
        for q in range(blocks):
            for a in range(COMP):
                at = a * PACK + q * GROUP
                out_ref[a, q] = out_ref[a, q] + acc[at : at + GROUP, :]

    for o in range(1, n_inst):
        inst_copy(o).wait_send()
    for c in to_up() + to_down():
        c.wait_send()

    @pl.when(r > 0)
    def _():
        for c in to_below():
            c.wait_send()

    @pl.when(r < n_row - 1)
    def _():
        for c in to_above():
            c.wait_send()


def per_device(
    direction,
    time_matrix,
    volume,
    diag_jac,
    face_jac,
    face_left,
    face_right,
    bound_jac,
    bound_cell,
    send_cell,
):
    n_inst = lax.axis_size("inst")
    n_row = lax.axis_size("row")
    n_pitch = lax.axis_size("pitch")
    cells = direction.shape[2]
    faces = face_left.shape[0]
    bounds = bound_cell.shape[1]
    blocks = cells // (GROUP * LANE)
    f_tiles = faces // LANE
    b_tiles = bounds // LANE
    width = 2 * faces + 5 * bounds
    f32, i32, bf16 = jnp.float32, jnp.int32, jnp.bfloat16
    cell_view = (blocks, GROUP, LANE)
    bound_view = (b_tiles, 4, LANE)
    hbm = pl.BlockSpec(memory_space=pl.ANY)

    def by_tile(cell):
        return cell.reshape(4, b_tiles, LANE).transpose(1, 0, 2)

    index_rows = pl.cdiv(b_tiles * 4, blocks * GROUP)
    assert index_rows * blocks * GROUP == b_tiles * 4
    result = pl.pallas_call(
        functools.partial(kernel, n_inst, n_row, n_pitch),
        out_shape=pltpu.VMEM((COMP, *cell_view), f32),
        in_specs=[hbm] * 10,
        out_specs=pl.BlockSpec(memory_space=pltpu.VMEM),
        scratch_shapes=[
            pltpu.SMEM((n_inst, n_inst), f32),
            pltpu.VMEM((COMP, *cell_view), f32),
            pltpu.VMEM((cells,), f32),
            pltpu.VMEM(cell_view, f32),
            pltpu.VMEM((25, *cell_view), f32),
            pltpu.VMEM((50, f_tiles, LANE), f32),
            pltpu.VMEM((f_tiles, LANE), i32),
            pltpu.VMEM((f_tiles, LANE), i32),
            pltpu.VMEM((50, *bound_view), f32),
            pltpu.VMEM(bound_view, i32),
            pltpu.VMEM(bound_view, i32),
            pltpu.VMEM((n_inst, COMP, *cell_view), f32),
            pltpu.VMEM((4, COMP + index_rows, *cell_view), f32),
            pltpu.VMEM((4, *bound_view), i32),
            pltpu.VMEM((25, b_tiles, LANE), f32),
            pltpu.VMEM((2 * bounds, LANE), bf16),
            pltpu.VMEM((COMP, *bound_view), f32),
            pltpu.VMEM((4, b_tiles, LANE), i32),
            pltpu.VMEM((TERMS, f_tiles, LANE), f32),
            pltpu.VMEM((4, TERMS, b_tiles, LANE), f32),
            pltpu.VMEM((TERMS * PACK, width), bf16),
            pltpu.VMEM((LANE, width), bf16),
            pltpu.VMEM((TERMS * PACK, LANE), f32),
            pltpu.SemaphoreType.DMA((1,)),
            pltpu.SemaphoreType.DMA((4,)),
            pltpu.SemaphoreType.REGULAR((3,)),
        ],
        compiler_params=pltpu.CompilerParams(collective_id=0, has_side_effects=True),
    )(
        time_matrix,
        direction[0].reshape(COMP, *cell_view),
        volume,
        diag_jac[0].reshape(25, *cell_view),
        face_jac[0].reshape(50, f_tiles, LANE),
        face_left.reshape(f_tiles, LANE),
        face_right.reshape(f_tiles, LANE),
        bound_jac[0].reshape(4, 50, b_tiles, LANE).transpose(1, 2, 0, 3),
        by_tile(bound_cell),
        by_tile(send_cell),
    )
    return result.reshape(1, COMP, cells)


def solution(mesh):
    return jax.shard_map(
        per_device,
        mesh=mesh,
        in_specs=(
            P("inst", None, ("row", "pitch")),
            P(),
            P(("row", "pitch")),
            P("inst", None, ("row", "pitch")),
            P("inst", None, ("row", "pitch")),
            P(("row", "pitch")),
            P(("row", "pitch")),
            P("inst", None, None, ("row", "pitch")),
            P(None, ("row", "pitch")),
            P(None, ("row", "pitch")),
        ),
        out_specs=P("inst", None, ("row", "pitch")),
        check_vma=False,
    )
```

```python
import functools
import jax
import jax.numpy as jnp
from jax import lax
from jax.experimental import pallas as pl
from jax.experimental.pallas import tpu as pltpu
from jax.sharding import PartitionSpec as P

LANE = 128
COMP = 5
TERMS = 2 * COMP
PACK = 16
GROUP = 4
MESH = pl.DeviceIdType.MESH


def gathered(own, cell):
    low = cell & (LANE - 1)
    high = cell >> 7
    chunks = own.shape[1] * GROUP
    masks = [high == h for h in range(chunks)]
    values = []
    for b in range(COMP):
        found = None
        for h in range(chunks):
            row = own[b, h // GROUP, pl.ds(h % GROUP, 1), :]
            part = jnp.take_along_axis(
                jnp.broadcast_to(row, cell.shape), low, axis=1, mode="promise_in_bounds"
            )
            found = part if h == 0 else jnp.where(masks[h], part, found)
        values.append(found)
    return values


def applied(block, base, values):
    result = []
    for a in range(COMP):
        total = None
        for b in range(COMP):
            term = block(base + COMP * a + b) * values[b]
            total = term if total is None else total + term
        result.append(total)
    return result


def two_terms(value):
    first = value.astype(jnp.bfloat16).astype(jnp.float32)
    return first, value - first


def packed_row(row):
    return jnp.broadcast_to(row, (PACK, LANE)).astype(jnp.bfloat16)


def hot_tile(hot, place, cell_row, value):
    low = packed_row((cell_row & (LANE - 1)).astype(jnp.float32))
    for s in range(0, LANE, PACK):
        index = lax.broadcasted_iota(jnp.int32, (PACK, LANE), 0) + s
        index = index.astype(jnp.float32).astype(jnp.bfloat16)
        hot[s : s + PACK, place : place + LANE] = jnp.where(
            index == low, jnp.bfloat16(value), jnp.bfloat16(0)
        )


def chunk_mask(cell_row):
    index = lax.broadcasted_iota(jnp.int32, (PACK, LANE), 0)
    index = index.astype(jnp.float32).astype(jnp.bfloat16)
    return index == packed_row((cell_row >> 7).astype(jnp.float32))


NEAR, LATE, BELOW, ABOVE = 0, 1, 2, 3
ORDER = (2, 3, 1, 0)


def kernel(n_inst, n_row, n_pitch, *refs):
    pl.run_scoped(
        functools.partial(body, n_inst, n_row, n_pitch, *refs),
        pltpu.SemaphoreType.DMA((10,)),
        pltpu.SemaphoreType.DMA((n_inst + 8,)),
    )


def body(
    n_inst,
    n_row,
    n_pitch,
    tm_hbm,
    dir_hbm,
    vol_hbm,
    diag_hbm,
    face_hbm,
    left_hbm,
    right_hbm,
    bound_hbm,
    bcell_hbm,
    scell_hbm,
    out_ref,
    tm_ref,
    own,
    vol_line,
    vol,
    diag,
    face,
    left,
    right,
    bound,
    bcell,
    scell,
    dirs,
    ghost,
    ghost_cell,
    late_jac,
    late_hot,
    late_value,
    picked,
    inner_flux,
    place_cell,
    flux_terms,
    bound_terms,
    rows,
    hot,
    acc,
    inst_recv,
    ghost_recv,
    ready,
    local_sem,
    send_sem,
):
    t = lax.axis_index("inst")
    r = lax.axis_index("row")
    p = lax.axis_index("pitch")
    blocks = own.shape[1]
    chunks = blocks * GROUP
    f_tiles = left.shape[0]
    faces = f_tiles * LANE
    b_tiles = bcell.shape[0]
    bounds = b_tiles * LANE
    last = n_inst - 1

    barrier = pltpu.get_barrier_semaphore()

    def signal(sem, **place):
        pl.semaphore_signal(sem, inc=1, device_id=place, device_id_type=MESH)

    up = lax.rem(p + 1, n_pitch)
    down = lax.rem(p + n_pitch - 1, n_pitch)

    down_first = jnp.logical_and(p >= 1, jnp.logical_or(p < n_pitch - 1, t > 0))
    up_first = jnp.logical_or(
        p == n_pitch - 1, jnp.logical_and(p == n_pitch - 2, t == 0)
    )

    @pl.when(jnp.logical_not(down_first))
    def _():
        signal(barrier, pitch=down)

    @pl.when(jnp.logical_not(up_first))
    def _():
        signal(barrier, pitch=up)

    pairs = [
        (dir_hbm, own),
        (bcell_hbm, bcell),
        (scell_hbm, scell),
        (left_hbm, left),
        (right_hbm, right),
        (face_hbm, face),
        (bound_hbm, bound),
        (diag_hbm, diag),
        (vol_hbm, vol_line),
        (tm_hbm, tm_ref),
    ]
    copies = [
        pltpu.make_async_copy(a, b, local_sem.at[i]) for i, (a, b) in enumerate(pairs)
    ]

    def ghost_copies(slot, at, early, **place):
        return [
            pltpu.make_async_remote_copy(
                src_ref=a,
                dst_ref=b,
                send_sem=send_sem.at[at + i],
                recv_sem=ghost_recv.at[slot],
                device_id=place,
                device_id_type=MESH,
            )
            for i, (a, b) in enumerate(
                [
                    (dir_hbm if early else own, ghost.at[slot, 0:COMP]),
                    (scell_hbm if early else scell, ghost_cell.at[slot]),
                ]
            )
        ]

    def to_up(early=False):
        slot = jnp.where(p == n_pitch - 1, LATE, NEAR)
        return ghost_copies(slot, n_inst, early, pitch=up)

    def to_down():
        slot = jnp.where(p == 1, NEAR, LATE)
        return ghost_copies(slot, n_inst + 2, False, pitch=down)

    def to_below():
        return ghost_copies(ABOVE, n_inst + 4, True, row=r - 1)

    def to_above():
        return ghost_copies(BELOW, n_inst + 6, False, row=r + 1)

    def start(group):
        for c in group:
            c.start()

    def inst_copy(o, early=False):
        return pltpu.make_async_remote_copy(
            src_ref=dir_hbm if early else own,
            dst_ref=dirs.at[o],
            send_sem=send_sem.at[o],
            recv_sem=inst_recv.at[0],
            device_id={"inst": lax.rem(t + o, n_inst)},
            device_id_type=MESH,
        )

    def inst_first(o):
        return jnp.logical_or(lax.rem(t + o, n_inst) == 0, t == last)

    leads = jnp.logical_and(p == n_pitch - 1, r == 0)
    first = jnp.logical_and(leads, t == 0)
    picks = jnp.logical_and(p == n_pitch - 1, r > 0)

    def picked_copy():
        return pltpu.make_async_remote_copy(
            src_ref=picked,
            dst_ref=late_value,
            send_sem=send_sem.at[n_inst],
            recv_sem=ghost_recv.at[LATE],
            device_id={"pitch": up},
            device_id_type=MESH,
        )


    @pl.when(first)
    def _():
        pl.semaphore_wait(barrier, 1)
        start(to_up(True))

    @pl.when(r < n_row - 1)
    def _():
        signal(barrier, row=r + 1)

    @pl.when(t == 0)
    def _():
        for u in range(1, n_inst):
            signal(barrier, inst=u)

    @pl.when(jnp.logical_and(t > 0, t < last))
    def _():
        signal(barrier, inst=last)

    greeted = jnp.where(t == last, last, jnp.where(t > 0, 1, 0))
    greeted = greeted + jnp.where(r > 0, 1, 0)
    greeted = greeted + jnp.where(down_first, 1, 0) + jnp.where(up_first, 1, 0)

    @pl.when(jnp.logical_and(greeted > 0, jnp.logical_not(first)))
    def _():
        pl.semaphore_wait(barrier, greeted)

    @pl.when(up_first)
    def _():
        signal(ready.at[1], pitch=up)

    @pl.when(jnp.logical_and(leads, jnp.logical_not(first)))
    def _():
        start(to_up(True))

    for o in range(1, n_inst):

        @pl.when(inst_first(o))
        def _(o=o):
            inst_copy(o, True).start()
            signal(ready.at[jnp.where(t == last, 2, 0)], inst=lax.rem(t + o, n_inst))

    @pl.when(down_first)
    def _():
        signal(ready.at[0], pitch=down)

    @pl.when(r > 0)
    def _():
        start(to_below())
        signal(ready.at[0], row=r - 1)

    start(copies)

    @pl.when(r == 0)
    def _():
        ghost[BELOW] = jnp.zeros(ghost.shape[1:], jnp.float32)
        ghost_cell[BELOW] = jnp.zeros(ghost_cell.shape[1:], jnp.int32)

    @pl.when(r == n_row - 1)
    def _():
        ghost[ABOVE] = jnp.zeros(ghost.shape[1:], jnp.float32)
        ghost_cell[ABOVE] = jnp.zeros(ghost_cell.shape[1:], jnp.int32)

    for c in copies[0:3]:
        c.wait()

    @pl.when(jnp.logical_and(up_first, p < n_pitch - 1))
    def _():
        start(to_up())

    @pl.when(picks)
    def _():
        for b, value in enumerate(gathered(own, scell[:, 1, :])):
            picked[b] = value

    @pl.when(down_first)
    def _():
        start(to_down())

    for c in copies[3:]:
        c.wait()

    @pl.when(picks)
    def _():
        picked_copy().start()

    def product(start, size):
        return lax.dot_general(
            rows[:, start : start + size],
            hot[:, start : start + size],
            (((1,), (1,)), ((), ())),
            preferred_element_type=jnp.float32,
        )

    total = None
    for g in range(0, f_tiles, 8):
        block = lambda i, g=g: face[i, g : g + 8, :]
        cell_l = left[g : g + 8, :]
        cell_r = right[g : g + 8, :]
        one = applied(block, 0, gathered(own, cell_l))
        two = applied(block, COMP * COMP, gathered(own, cell_r))
        for a in range(COMP):
            first, rest = two_terms(one[a] + two[a])
            flux_terms[a, g : g + 8, :] = first
            flux_terms[COMP + a, g : g + 8, :] = rest
        for s in range(g, g + 8):
            place = 2 * s * LANE
            row_l = left[s : s + 1, :]
            row_r = right[s : s + 1, :]
            hot_tile(hot, place, row_l, 1.0)
            hot_tile(hot, place + LANE, row_r, -1.0)
            mask_l = chunk_mask(row_l)
            mask_r = chunk_mask(row_r)
            for a in range(TERMS):
                value = packed_row(flux_terms[a, s : s + 1, :])
                at = slice(a * PACK, (a + 1) * PACK)
                zero = jnp.bfloat16(0)
                rows[at, place : place + LANE] = jnp.where(mask_l, value, zero)
                rows[at, place + LANE : place + 2 * LANE] = jnp.where(mask_r, value, zero)
        part = product(2 * g * LANE, 16 * LANE)
        total = part if total is None else total + part
    acc[...] = total

    edge = p == 0

    def side(slot, pick):
        if slot >= BELOW:
            return pick(slot)
        if slot == NEAR:
            return jnp.where(edge, pick(1), pick(0))
        return jnp.where(edge, pick(0), pick(1))

    def boundary_place(slot, j):
        return 2 * faces + (ORDER[slot] * b_tiles + j) * LANE

    for j in range(b_tiles):
        block = lambda i, j=j: bound[i, j]
        flux = applied(block, 0, gathered(own, bcell[j]))
        for a in range(COMP):
            inner_flux[a, j] = flux[a]
    for slot in range(4):
        place_cell[slot] = side(slot, lambda k: bcell[:, k, :])
        for j in range(b_tiles):
            place = boundary_place(slot, j)
            hot_tile(hot, place, place_cell[slot, j : j + 1, :], 1.0)
            if slot == LATE:
                turned = hot[:, place : place + LANE].astype(jnp.float32).T
                turned = turned.astype(jnp.bfloat16)
                late_hot[j * LANE : (j + 1) * LANE, :] = turned
                late_hot[bounds + j * LANE : bounds + (j + 1) * LANE, :] = turned
    for i in range(COMP * COMP):
        late_jac[i] = side(LATE, lambda k, i=i: bound[COMP * COMP + i, :, k, :])

    for h in range(chunks):
        vol[h // GROUP, pl.ds(h % GROUP, 1), :] = vol_line[
            h * LANE : (h + 1) * LANE
        ].reshape(1, LANE)

    for q in range(blocks):
        local = applied(lambda i, q=q: diag[i, q], 0, [own[b, q] for b in range(COMP)])
        for a in range(COMP):
            out_ref[a, q] = local[a] + (tm_ref[t, t] * own[a, q]) * vol[q]

    answered = jnp.where(t == 0, max(n_inst - 2, 0), 0)
    answered = answered + jnp.where(r < n_row - 1, 1, 0)
    answered = answered + jnp.where(up_first, 0, 1)

    @pl.when(answered > 0)
    def _():
        pl.semaphore_wait(ready.at[0], answered)

    @pl.when(t == 0)
    def _():
        for o in range(1, last):
            inst_copy(o).start()

    @pl.when(r < n_row - 1)
    def _():
        start(to_above())

    @pl.when(jnp.logical_not(up_first))
    def _():
        start(to_up())

    def answer_down():
        pl.semaphore_wait(ready.at[1], 1)
        start(to_down())

    @pl.when(jnp.logical_and(p > 0, jnp.logical_not(down_first)))
    def _():
        answer_down()

    @pl.when(t < last)
    def _():
        pl.semaphore_wait(ready.at[2], 1)
        for o in range(1, n_inst):
            u = lax.rem(t + o, n_inst)

            @pl.when(jnp.logical_or(u == last, jnp.logical_and(t > 0, u > 0)))
            def _(o=o):
                inst_copy(o).start()

    @pl.when(p == 0)
    def _():
        answer_down()

    def arrived(slot):
        pltpu.make_async_copy(ghost.at[slot], ghost.at[slot], ghost_recv.at[slot]).wait()

    def ghost_values(slot):
        cell = side(slot, lambda k: ghost_cell[slot, :, k ^ 1, :])
        return gathered(ghost.at[slot], cell)

    def boundary(slot, values):
        total = [side(slot, lambda k, a=a: inner_flux[a, :, k, :]) for a in range(COMP)]
        for b, value in enumerate(values):
            for a in range(COMP):
                i = COMP * a + b
                if slot == LATE:
                    block = late_jac[i]
                else:
                    block = side(slot, lambda k: bound[COMP * COMP + i, :, k, :])
                total[a] = total[a] + block * value
        for a in range(COMP):
            first, rest = two_terms(total[a])
            bound_terms[slot, a] = first
            bound_terms[slot, COMP + a] = rest
        for j in range(b_tiles):
            mask = chunk_mask(place_cell[slot, j : j + 1, :])
            for a in range(TERMS):
                value = packed_row(bound_terms[slot, a, j : j + 1, :])
                term, place = a, boundary_place(slot, j)
                if slot == LATE and a >= COMP:
                    term, place = a - COMP, place + bounds
                rows[term * PACK : (term + 1) * PACK, place : place + LANE] = jnp.where(
                    mask, value, jnp.bfloat16(0)
                )

    def late_product():
        at = slice(boundary_place(LATE, 0), boundary_place(LATE, 0) + 2 * bounds)
        return lax.dot_general(
            rows[0 : COMP * PACK, at],
            late_hot[...],
            (((1,), (0,)), ((), ())),
            preferred_element_type=jnp.float32,
        )

    @pl.when(r > 0)
    def _():
        arrived(BELOW)

    @pl.when(r < n_row - 1)
    def _():
        arrived(ABOVE)

    boundary(ABOVE, ghost_values(ABOVE))
    boundary(BELOW, ghost_values(BELOW))
    acc[...] = acc[...] + product(2 * faces, 2 * bounds)

    arrived(NEAR)
    boundary(NEAR, ghost_values(NEAR))
    acc[...] = acc[...] + product(boundary_place(NEAR, 0), bounds)

    @pl.when(p > 0)
    def _():
        arrived(LATE)
        boundary(LATE, ghost_values(LATE))
        acc[0 : COMP * PACK] = acc[0 : COMP * PACK] + late_product()

    if n_inst > 1:
        others = dirs.at[1:n_inst]
        pltpu.make_async_copy(others, others, inst_recv.at[0]).wait()
    weights = [tm_ref[t, lax.rem(t + n_inst - o, n_inst)] for o in range(1, n_inst)]
    for q in range(blocks):
        for a in range(COMP):
            at = a * PACK + q * GROUP
            both = acc[at : at + GROUP, :]
            at = at + COMP * PACK
            both = both + acc[at : at + GROUP, :]
            mixed = None
            for o in range(1, n_inst):
                term = weights[o - 1] * dirs[o, a, q]
                mixed = term if mixed is None else mixed + term
            if mixed is not None:
                both = mixed * vol[q] + both
            out_ref[a, q] = out_ref[a, q] + both

    @pl.when(p == 0)
    def _():
        @pl.when(r == 0)
        def _():
            arrived(LATE)
            for b, value in enumerate(ghost_values(LATE)):
                late_value[b] = value

        @pl.when(r > 0)
        def _():
            pltpu.make_async_copy(late_value, late_value, ghost_recv.at[LATE]).wait()

        boundary(LATE, [late_value[b] for b in range(COMP)])
        acc[0 : COMP * PACK] = late_product()
        for q in range(blocks):
            for a in range(COMP):
                at = a * PACK + q * GROUP
                out_ref[a, q] = out_ref[a, q] + acc[at : at + GROUP, :]

    for o in range(1, n_inst):
        inst_copy(o).wait_send()
    for c in to_down():
        c.wait_send()

    @pl.when(jnp.logical_not(picks))
    def _():
        for c in to_up():
            c.wait_send()

    @pl.when(picks)
    def _():
        picked_copy().wait_send()

    @pl.when(r > 0)
    def _():
        for c in to_below():
            c.wait_send()

    @pl.when(r < n_row - 1)
    def _():
        for c in to_above():
            c.wait_send()


def per_device(
    direction,
    time_matrix,
    volume,
    diag_jac,
    face_jac,
    face_left,
    face_right,
    bound_jac,
    bound_cell,
    send_cell,
):
    n_inst = lax.axis_size("inst")
    n_row = lax.axis_size("row")
    n_pitch = lax.axis_size("pitch")
    cells = direction.shape[2]
    faces = face_left.shape[0]
    bounds = bound_cell.shape[1]
    blocks = cells // (GROUP * LANE)
    f_tiles = faces // LANE
    b_tiles = bounds // LANE
    width = 2 * faces + 5 * bounds
    f32, i32, bf16 = jnp.float32, jnp.int32, jnp.bfloat16
    cell_view = (blocks, GROUP, LANE)
    bound_view = (b_tiles, 4, LANE)
    hbm = pl.BlockSpec(memory_space=pl.ANY)

    def by_tile(cell):
        return cell.reshape(4, b_tiles, LANE).transpose(1, 0, 2)

    index_rows = pl.cdiv(b_tiles * 4, blocks * GROUP)
    assert index_rows * blocks * GROUP == b_tiles * 4
    result = pl.pallas_call(
        functools.partial(kernel, n_inst, n_row, n_pitch),
        out_shape=pltpu.VMEM((COMP, *cell_view), f32),
        in_specs=[hbm] * 10,
        out_specs=pl.BlockSpec(memory_space=pltpu.VMEM),
        scratch_shapes=[
            pltpu.SMEM((n_inst, n_inst), f32),
            pltpu.VMEM((COMP, *cell_view), f32),
            pltpu.VMEM((cells,), f32),
            pltpu.VMEM(cell_view, f32),
            pltpu.VMEM((25, *cell_view), f32),
            pltpu.VMEM((50, f_tiles, LANE), f32),
            pltpu.VMEM((f_tiles, LANE), i32),
            pltpu.VMEM((f_tiles, LANE), i32),
            pltpu.VMEM((50, *bound_view), f32),
            pltpu.VMEM(bound_view, i32),
            pltpu.VMEM(bound_view, i32),
            pltpu.VMEM((n_inst, COMP, *cell_view), f32),
            pltpu.VMEM((4, COMP + index_rows, *cell_view), f32),
            pltpu.VMEM((4, *bound_view), i32),
            pltpu.VMEM((25, b_tiles, LANE), f32),
            pltpu.VMEM((2 * bounds, LANE), bf16),
            pltpu.VMEM((COMP, b_tiles, LANE), f32),
            pltpu.VMEM((COMP, b_tiles, LANE), f32),
            pltpu.VMEM((COMP, *bound_view), f32),
            pltpu.VMEM((4, b_tiles, LANE), i32),
            pltpu.VMEM((TERMS, f_tiles, LANE), f32),
            pltpu.VMEM((4, TERMS, b_tiles, LANE), f32),
            pltpu.VMEM((TERMS * PACK, width), bf16),
            pltpu.VMEM((LANE, width), bf16),
            pltpu.VMEM((TERMS * PACK, LANE), f32),
            pltpu.SemaphoreType.DMA((1,)),
            pltpu.SemaphoreType.DMA((4,)),
            pltpu.SemaphoreType.REGULAR((3,)),
        ],
        compiler_params=pltpu.CompilerParams(collective_id=0, has_side_effects=True),
    )(
        time_matrix,
        direction[0].reshape(COMP, *cell_view),
        volume,
        diag_jac[0].reshape(25, *cell_view),
        face_jac[0].reshape(50, f_tiles, LANE),
        face_left.reshape(f_tiles, LANE),
        face_right.reshape(f_tiles, LANE),
        bound_jac[0].reshape(4, 50, b_tiles, LANE).transpose(1, 2, 0, 3),
        by_tile(bound_cell),
        by_tile(send_cell),
    )
    return result.reshape(1, COMP, cells)


def solution(mesh):
    return jax.shard_map(
        per_device,
        mesh=mesh,
        in_specs=(
            P("inst", None, ("row", "pitch")),
            P(),
            P(("row", "pitch")),
            P("inst", None, ("row", "pitch")),
            P("inst", None, ("row", "pitch")),
            P(("row", "pitch")),
            P(("row", "pitch")),
            P("inst", None, None, ("row", "pitch")),
            P(None, ("row", "pitch")),
            P(None, ("row", "pitch")),
        ),
        out_specs=P("inst", None, ("row", "pitch")),
        check_vma=False,
    )
```
